1024 devices in a mesh: batch: 8 (over x_hi, core), heads: 8 (over z), seq: 16 (over x_lo, y).
Axes of the slice: x: 8 (x_hi: 4, x_lo: 2; x = x_hi * 2 + x_lo), y: 8, z: 8, core: 2. Of those that a mesh axis runs over, the one named last changes fastest.
Arguments:
- tokens: bfloat16 [8, 2048, 1536], P('batch', 'seq'), may hold values from -24 to 24
- conv_taps: float32 [5, 1536], replicated, may hold values from -2.5 to 2.5
- w_query: bfloat16 [1536, 1024], P(None, 'heads')
- w_key: bfloat16 [1536, 1024], P(None, 'heads')
- w_value: bfloat16 [1536, 1536], P(None, 'heads'), may hold values from -0.15625 to 0.15625
- grad_out: bfloat16 [8, 2048, 1536], P('batch', 'seq', 'heads'), may hold values from -4 to 4
Outputs:
- attended: bfloat16 [8, 2048, 1536], P('batch', 'seq', 'heads')
- grad_tokens: float32 [8, 2048, 1536], P('batch', 'seq', 'heads')
- grad_query: float32 [1536, 1024], P(('batch', 'seq'), 'heads')
- grad_key: float32 [1536, 1024], P(('batch', 'seq'), 'heads')
- grad_value: float32 [1536, 1536], P(('batch', 'seq'), 'heads')
The draws below stay inside these ranges and needn't reach their ends.
All inputs are finite; a program needn't handle non-finite values.
Results may differ from the reference program's by a relative error of at most 0.02.
The reference program's roundings to bfloat16 on the way count: a program that leaves them out, or rounds other values in their place, can miss the bound.
Values may be sent and summed in bfloat16 or wider, within the bound.
No kernel may reach another device: no remote copies, remote signals or barrier semaphores. Data moves between devices by JAX's collectives and lax.ppermute only.
A program may use at most 32 MiB of HBM per device.

```python
import math
import jax
import jax.numpy as jnp
from jax import lax

D = 1536
DH = 128
DV = 192
DILATION_STEP = 4
S_DEV = 128
HEADS = 8
SEQ = 2048
B = 8


def draw_tokens(key, part):
    normal_rows = jnp.clip(jax.random.normal(jax.random.fold_in(key, 101), (B, SEQ, D), jnp.float32), -4.0, 4.0)
    return normal_rows.astype(jnp.bfloat16)


def shared_base(key):
    return jnp.clip(jax.random.normal(jax.random.fold_in(key, 201), (D, HEADS * DH), jnp.float32), -4.0, 4.0)


def draw_w_query(key, part):
    return (1.8 * shared_base(key) / math.sqrt(D)).astype(jnp.bfloat16)


def draw_w_key(key, part):
    second = jnp.clip(jax.random.normal(jax.random.fold_in(key, 202), (D, HEADS * DH), jnp.float32), -4.0, 4.0)
    return (second / math.sqrt(D)).astype(jnp.bfloat16)


def level_of(key, dims, cuts, low, top_value):
    gain, own = 1.0, jax.random.fold_in(key, 6)
    for axis_at, blocks in cuts:
        heights = jnp.exp(jax.random.uniform(jax.random.fold_in(own, axis_at), (blocks,), jnp.float32, low / len(cuts), top_value / len(cuts)))
        gain = gain * jnp.repeat(heights, dims[axis_at] // blocks).reshape([-1 if axis == axis_at else 1 for axis in range(len(dims))])
    return gain


def bell_draw(own_key, extent, scale, reach, shards=(), held_as=jnp.bfloat16):
    values = jax.random.normal(own_key, extent, jnp.float32) * scale
    if len(shards) > 0:
        values = level_of(own_key, extent, shards, -0.22, 0.18) * values
    return jnp.clip(values, min=-reach, max=reach).astype(held_as)


def setup_inputs(seed: int = 0) -> dict:
    key_of = jax.random.split(jax.random.key(seed), 7)
    return {
        "tokens": draw_tokens(jax.random.fold_in(key_of[6], 71), 0),
        "conv_taps": bell_draw(key_of[1], (5, D), 0.5, 2.5, (), jnp.float32),
        "w_query": draw_w_query(jax.random.fold_in(key_of[6], 71), 0),
        "w_key": draw_w_key(jax.random.fold_in(key_of[6], 71), 0),
        "w_value": bell_draw(key_of[4], (D, HEADS * DV), D ** -0.5, 0.15625, ((1, 8),)),
        "grad_out": bell_draw(key_of[5], (B, SEQ, HEADS * DV), 1.0, 4.0, ((0, 8), (1, 16), (2, 8))),
    }


def dilated(signal, kernel, shift_direction):
    border_rows = 2 * DILATION_STEP
    padded = jnp.pad(signal, ((0, 0), (border_rows, border_rows), (0, 0)))
    summed = signal
    for kernel_tap_index in range(5):
        tap_offset = shift_direction * DILATION_STEP * (kernel_tap_index - 2)
        summed = summed + kernel[kernel_tap_index] * padded[:, border_rows + tap_offset:border_rows + tap_offset + SEQ, :]
    return summed

def block_terms(left_rows, right_rows, right_width):
    blocks = SEQ // S_DEV
    left_blocks = left_rows.astype(jnp.float32).reshape(blocks, S_DEV, SEQ)
    right_blocks = right_rows.astype(jnp.float32).reshape(blocks, S_DEV, right_width)
    rounded = jnp.einsum('nik,nid->nkd', left_blocks, right_blocks).astype(jnp.bfloat16)
    rounded = lax.optimization_barrier(rounded)
    return lax.optimization_barrier(jnp.sum(rounded.astype(jnp.float32), axis=0)).astype(jnp.bfloat16)

def head_pass(operands):
    queries, key_rows, value_rows, out_grads = operands
    score_scale = 1.0 / math.sqrt(DH)
    logits = jnp.dot(queries, key_rows.T, preferred_element_type=jnp.float32) * score_scale
    highest = lax.optimization_barrier(jnp.max(logits, axis=1, keepdims=True))
    exponents = jnp.exp(logits - highest)
    attention = exponents / lax.optimization_barrier(jnp.sum(exponents, axis=1, keepdims=True))
    attention_b = attention.astype(jnp.bfloat16)
    attended = jnp.dot(attention_b, value_rows, preferred_element_type=jnp.float32).astype(jnp.bfloat16)
    attention_grads = jnp.dot(out_grads, value_rows.T, preferred_element_type=jnp.float32)
    row_dots = lax.optimization_barrier(jnp.sum(attention * attention_grads, axis=1, keepdims=True))
    logit_grads = (attention * (attention_grads - row_dots) * score_scale).astype(jnp.bfloat16)
    query_grads = jnp.dot(logit_grads, key_rows, preferred_element_type=jnp.float32).astype(jnp.bfloat16)
    key_grads = block_terms(logit_grads, queries, DH)
    value_grads = block_terms(attention_b, out_grads, DV)
    return (attended, query_grads, key_grads, value_grads)

def per_head(array, head_width):
    return array.reshape(B, SEQ, HEADS, head_width).transpose(0, 2, 1, 3).reshape(B * HEADS, SEQ, head_width)

def joined(array, head_width):
    return array.reshape(B, HEADS, SEQ, head_width).transpose(0, 2, 1, 3).reshape(B, SEQ, HEADS * head_width)

def reference(tokens, conv_taps, w_query, w_key, w_value, grad_out):
    blended = dilated(tokens.astype(jnp.float32), conv_taps, 1).astype(jnp.bfloat16)
    flat_rows = blended.reshape(B * SEQ, D)
    queries = jnp.dot(flat_rows, w_query, preferred_element_type=jnp.float32).astype(jnp.bfloat16)
    key_rows = jnp.dot(flat_rows, w_key, preferred_element_type=jnp.float32).astype(jnp.bfloat16)
    value_rows = jnp.dot(flat_rows, w_value, preferred_element_type=jnp.float32).astype(jnp.bfloat16)
    operands = (per_head(queries, DH), per_head(key_rows, DH), per_head(value_rows, DV), per_head(grad_out, DV))
    attended, query_grads, key_grads, value_grads = lax.map(head_pass, operands)
    query_flat = joined(query_grads, DH).reshape(B * SEQ, HEADS * DH)
    key_flat = joined(key_grads, DH).reshape(B * SEQ, HEADS * DH)
    value_flat = joined(value_grads, DV).reshape(B * SEQ, HEADS * DV)
    feature_sum = jnp.dot(query_flat, w_query.T, preferred_element_type=jnp.float32)
    feature_sum = feature_sum + jnp.dot(key_flat, w_key.T, preferred_element_type=jnp.float32)
    feature_sum = feature_sum + jnp.dot(value_flat, w_value.T, preferred_element_type=jnp.float32)
    feature_grads = lax.optimization_barrier(feature_sum.astype(jnp.bfloat16))
    grad_tokens = dilated(feature_grads.reshape(B, SEQ, D).astype(jnp.float32), conv_taps, -1)
    grad_scale = 1.0 / math.sqrt(B * SEQ)
    grad_query = jnp.dot(flat_rows.T, query_flat, preferred_element_type=jnp.float32) * grad_scale
    grad_key = jnp.dot(flat_rows.T, key_flat, preferred_element_type=jnp.float32) * grad_scale
    grad_value = jnp.dot(flat_rows.T, value_flat, preferred_element_type=jnp.float32) * grad_scale
    return (joined(attended, DV), grad_tokens, grad_query, grad_key, grad_value)
```

```python
import math

import jax
import jax.numpy as jnp
from jax import lax
from jax.experimental import pallas as pl
from jax.experimental.pallas import tpu as pltpu
from jax.sharding import Mesh
from jax.sharding import PartitionSpec as P

DH = 128
DV = 192
DILATION_STEP = 4
REACH = 2 * DILATION_STEP
PAD = 16
VMEM = 16 << 20

F32 = jnp.float32
BF16 = jnp.bfloat16
SEQ = ("sx", "yh", "yl")
QGROUP = ("sx", "yl")
KGROUP = "yh"
PAIR = ("core", "sx")
REST = ("bx", "yh", "yl")


def dot(a, b, ca, cb):
    return lax.dot_general(a, b, (((ca,), (cb,)), ((), ())), preferred_element_type=F32)


def call(body, outs, *args, name):
    def kernel(*refs):
        body(refs[: len(args)], refs[len(args) :])

    return pl.pallas_call(
        kernel,
        out_shape=[jax.ShapeDtypeStruct(s, t) for s, t in outs],
        name=name,
        compiler_params=pltpu.CompilerParams(vmem_limit_bytes=VMEM),
    )(*args)


def exchange(x, axis):
    return lax.all_to_all(x, axis, split_axis=0, concat_axis=0, tiled=True)


def shift_pair(low_source, high_source, axes):
    count = lax.axis_size(axes)
    forward = [(i, i + 1) for i in range(count - 1)]
    backward = [(j, i) for i, j in forward]
    return lax.ppermute(low_source, axes, forward), lax.ppermute(high_source, axes, backward)


def project(ins, outs):
    tokens, low, high, taps, wq, wk, wvt = ins
    blended_out, q_out, kv_out = outs
    rows = tokens.shape[0]
    body = tokens[...].astype(F32)
    padded = jnp.concatenate([low[...].astype(F32), body, high[...].astype(F32)], axis=0)
    summed = body
    for t in range(5):
        summed = summed + taps[t : t + 1, :] * padded[t * DILATION_STEP : t * DILATION_STEP + rows]
    blended = summed.astype(BF16)
    blended_out[...] = blended
    qt = dot(blended, wq[...], 1, 0).T.astype(BF16)
    kt = dot(blended, wk[...], 1, 0).T.astype(BF16)
    vt = dot(wvt[...], blended, 1, 1).astype(BF16)
    for m in range(q_out.shape[0]):
        q_out[m] = qt
    for n in range(kv_out.shape[0]):
        kv_out[n, :DH] = kt
        kv_out[n, DH:] = vt


def lanes(ref, first, last):
    return jnp.concatenate([ref[n, first:last] for n in range(ref.shape[0])], axis=1)


SCALE = 1.0 / math.sqrt(DH)


def statistics(ins, outs):
    kv, q, do = ins
    (stats,) = outs
    k_rows = lanes(kv, 0, DH).T
    v_rows = lanes(kv, DH, DH + DV).T
    width = q.shape[2]
    blocks = q.shape[0]
    for m in range(blocks):
        s = dot(k_rows, q[m], 1, 0) * SCALE
        top = jnp.max(s, axis=0, keepdims=True)
        e = jnp.exp(s - top)
        total = jnp.sum(e, axis=0, keepdims=True)
        dp = dot(v_rows, do[m], 1, 0)
        weighted = jnp.sum(e * dp, axis=0, keepdims=True)
        part = jnp.concatenate([top, total, weighted, jnp.zeros((5, width), F32)], axis=0)
        for c in range(stats.shape[0]):
            stats[c, :, m * width : (m + 1) * width] = part


def attend(ins, outs):
    kv, q, do, stats = ins
    odq, dkv = outs
    kt = lanes(kv, 0, DH)
    vt = lanes(kv, DH, DH + DV)
    k_rows = kt.T
    v_rows = vt.T
    width = q.shape[2]
    dk = dv = None
    for m in range(q.shape[0]):
        part = [stats[c, :, m * width : (m + 1) * width] for c in range(stats.shape[0])]
        top = part[0][0:1]
        for x in part[1:]:
            top = jnp.maximum(top, x[0:1])
        total = jnp.zeros_like(top)
        weighted = jnp.zeros_like(top)
        for x in part:
            factor = jnp.exp(x[0:1] - top)
            total = total + factor * x[1:2]
            weighted = weighted + factor * x[2:3]
        row_dots = weighted / total
        s = dot(k_rows, q[m], 1, 0) * SCALE
        a = jnp.exp(s - top) / total
        ab = a.astype(BF16)
        dp = dot(v_rows, do[m], 1, 0)
        ds = (a * (dp - row_dots) * SCALE).astype(BF16)
        odq[m, :DV] = dot(vt, ab, 1, 0).astype(BF16)
        odq[m, DV:] = dot(kt, ds, 1, 0).astype(BF16)
        dk_m = dot(q[m], ds, 1, 1)
        dv_m = dot(do[m], ab, 1, 1)
        dk = dk_m if dk is None else dk + dk_m
        dv = dv_m if dv is None else dv + dv_m
    for n in range(dkv.shape[0]):
        dkv[n, :DH] = dk[:, n * width : (n + 1) * width].astype(BF16)
        dkv[n, DH:] = dv[:, n * width : (n + 1) * width].astype(BF16)


def add_up(ref):
    total = ref[0].astype(F32)
    for n in range(1, ref.shape[0]):
        total = total + ref[n].astype(F32)
    return total


def features(ins, outs):
    odq, dkv, wq, wk, wv = ins
    attended, grads, feature = outs
    first = add_up(odq)
    second = add_up(dkv).astype(BF16)
    attended[...] = first[:DV].astype(BF16)
    dq = first[DV:].astype(BF16)
    for n in range(grads.shape[0]):
        grads[n, :DH] = dq
        grads[n, DH:] = second
    total = dot(wq[...], dq, 1, 0) + dot(wk[...], second[:DH], 1, 0)
    total = total + dot(wv[...], second[DH:], 1, 0)
    feature[...] = total.astype(BF16)


def outer(ins, outs):
    left, right = ins
    total = dot(left[0], right[0], 1, 1)
    for n in range(1, left.shape[0]):
        total = total + dot(left[n], right[n], 1, 1)
    outs[0][...] = total.astype(BF16)


def weight_sum(ins, outs, scale):
    total = add_up(ins[0]) * scale
    rows = outs[0].shape[0]
    outs[0][...] = total[:rows, :DH]
    outs[1][...] = total[:rows, DH : 2 * DH]
    outs[2][...] = total[:rows, 2 * DH :]


def feature_sum(ins, outs):
    outs[0][...] = add_up(ins[0]).astype(BF16)


def spread(ins, outs):
    own, low, high, taps = ins
    width = own.shape[1]
    body = own[...].astype(F32)
    padded = jnp.concatenate([low[...].astype(F32), body, high[...].astype(F32)], axis=1)
    summed = body
    for t in range(5):
        start = width - (t - 2) * DILATION_STEP
        summed = summed + taps[:, t : t + 1] * padded[:, start : start + width]
    outs[0][...] = summed


def local(tokens, conv_taps, w_query, w_key, w_value, grad_out):
    x = tokens[0]
    rows, columns = x.shape
    q_count = lax.axis_size(QGROUP)
    k_count = lax.axis_size(KGROUP)
    pair_count = lax.axis_size(PAIR)
    bx, core, sx = (lax.axis_size(a) for a in ("bx", "core", "sx"))
    y = lax.axis_size(("yh", "yl"))
    rest = bx * y
    share = columns // (bx * core * sx * y)
    heads = lax.axis_size("heads")
    slice_width = columns // heads

    out_grads = jnp.broadcast_to(grad_out[0].T[None], (q_count, DV, rows))
    do = exchange(out_grads, QGROUP)
    low, high = shift_pair(x[rows - REACH :], x[:REACH], SEQ)
    blended, q_all, kv_all = call(
        project,
        [((rows, columns), BF16), ((q_count, DH, rows), BF16), ((k_count, DH + DV, rows), BF16)],
        x, low, high, conv_taps, w_query, w_key, w_value.T,
        name="project",
    )
    kv = exchange(kv_all, KGROUP)
    q = exchange(q_all, QGROUP)

    groups = blended.reshape(rows, bx, core, sx, y, share)
    groups = jnp.pad(groups, ((0, 0),) * 5 + ((0, PAD - share),))
    groups = groups.transpose(2, 3, 1, 4, 5, 0).reshape(pair_count, rest * PAD, rows)
    left = exchange(groups, PAIR)

    (stats,) = call(
        statistics, [((q_count, 8, q_count * rows), F32)], kv, q, do, name="statistics"
    )
    stats = exchange(stats, QGROUP)
    odq, dkv = call(
        attend,
        [((q_count, DH + DV, rows), BF16), ((k_count, DH + DV, rows), BF16)],
        kv, q, do, stats,
        name="attend",
    )
    dkv = exchange(dkv, KGROUP)
    odq = exchange(odq, QGROUP)
    attended, grads, feature = call(
        features,
        [
            ((DV, rows), BF16),
            ((pair_count, 2 * DH + DV, rows), BF16),
            ((columns, rows), BF16),
        ],
        odq, dkv, w_query, w_key, w_value,
        name="features",
    )
    right = exchange(grads, PAIR)
    feature = exchange(feature.reshape(heads, slice_width, rows), "heads")
    (product,) = call(
        outer, [((rest * PAD, 2 * DH + DV), BF16)], left, right, name="outer"
    )
    product = exchange(product.reshape(rest, PAD, 2 * DH + DV), REST)

    (own,) = call(feature_sum, [((slice_width, rows), BF16)], feature, name="feature_sum")
    before, after = shift_pair(own, own, SEQ)
    taps = lax.dynamic_slice_in_dim(
        conv_taps, lax.axis_index("heads") * slice_width, slice_width, 1
    ).T
    (grad_tokens,) = call(
        spread, [((slice_width, rows), F32)], own, before, after, taps, name="spread"
    )
    scale = 1.0 / math.sqrt(bx * core * sx * y * rows)
    grad_query, grad_key, grad_value = call(
        lambda i, o: weight_sum(i, o, scale),
        [((share, DH), F32), ((share, DH), F32), ((share, DV), F32)],
        product,
        name="weight_sum",
    )
    return attended.T[None], grad_tokens.T[None], grad_query, grad_key, grad_value


def split(mesh):
    batch, heads, seq = mesh.devices.shape
    shape = (batch // 2, 2, heads, 2, seq // 4, 2)
    return Mesh(mesh.devices.reshape(shape), ("bx", "core", "heads", "sx", "yh", "yl"))


def solution(mesh):
    batch = ("bx", "core")
    return jax.shard_map(
        local,
        mesh=split(mesh),
        in_specs=(
            P(batch, SEQ, None),
            P(),
            P(None, "heads"),
            P(None, "heads"),
            P(None, "heads"),
            P(batch, SEQ, "heads"),
        ),
        out_specs=(
            P(batch, SEQ, "heads"),
            P(batch, SEQ, "heads"),
            P(batch + SEQ, "heads"),
            P(batch + SEQ, "heads"),
            P(batch + SEQ, "heads"),
        ),
        check_vma=False,
    )
```

```python
import math

import jax
import jax.numpy as jnp
from jax import lax
from jax.experimental import pallas as pl
from jax.experimental.pallas import tpu as pltpu
from jax.sharding import Mesh
from jax.sharding import PartitionSpec as P

DH = 128
DV = 192
DILATION_STEP = 4
REACH = 2 * DILATION_STEP
PAD = 16
VMEM = 16 << 20

F32 = jnp.float32
BF16 = jnp.bfloat16
SEQ = ("sx", "yh", "yl")
QGROUP = ("sx", "yl")
KGROUP = "yh"
PAIR = ("core", "sx")
REST = ("bx", "yh", "yl")


def dot(a, b, ca, cb):
    return lax.dot_general(a, b, (((ca,), (cb,)), ((), ())), preferred_element_type=F32)


def call(body, outs, *args, far=0, vmem=VMEM):
    count = len(args)

    def kernel(*refs):
        ins, results = refs[:count], refs[count : count + len(outs)]
        if far:
            held, sems = refs[-1 - far : -1], refs[-1]
            copies = [
                pltpu.make_async_copy(ins[i], held[i], sems.at[i]) for i in range(far)
            ]
            for c in copies:
                c.start()
            body(tuple(held) + ins[far:], results, copies)
        else:
            body(ins, results)

    scratch = [pltpu.VMEM(a.shape, a.dtype) for a in args[:far]]
    if far:
        scratch.append(pltpu.SemaphoreType.DMA((far,)))
    return pl.pallas_call(
        kernel,
        out_shape=[jax.ShapeDtypeStruct(s, t) for s, t in outs],
        in_specs=[pl.BlockSpec(memory_space=pltpu.HBM)] * far
        + [pl.BlockSpec(memory_space=pltpu.VMEM)] * (count - far),
        scratch_shapes=scratch,
        compiler_params=pltpu.CompilerParams(vmem_limit_bytes=vmem),
    )(*args)


def exchange(x, axis):
    return lax.all_to_all(x, axis, split_axis=0, concat_axis=0, tiled=True)


def swap(x, axes, k):
    count = lax.axis_size(axes)
    return lax.ppermute(x, axes, [(i, i ^ k) for i in range(count)])


def gather(x, axes):
    return [x] + [swap(x, axes, k) for k in range(1, lax.axis_size(axes))]


def trade(pieces, axes):
    return [pieces[0]] + [swap(pieces[k], axes, k) for k in range(1, lax.axis_size(axes))]


def shift_pair(low_source, high_source, axes):
    count = lax.axis_size(axes)
    forward = [(i, i + 1) for i in range(count - 1)]
    backward = [(j, i) for i, j in forward]
    return lax.ppermute(low_source, axes, forward), lax.ppermute(high_source, axes, backward)


def project(ins, outs, copies):
    tokens, wq, wk, wvt, low, high, taps = ins
    blended_out, qt, kv_out = outs
    rows = tokens.shape[0]
    copies[0].wait()
    body = tokens[...].astype(F32)
    padded = jnp.concatenate([low[...].astype(F32), body, high[...].astype(F32)], axis=0)
    summed = body
    for t in range(5):
        summed = summed + taps[t : t + 1, :] * padded[t * DILATION_STEP : t * DILATION_STEP + rows]
    blended = summed.astype(BF16)
    blended_out[...] = blended
    copies[1].wait()
    qt[...] = dot(blended, wq[...], 1, 0).T.astype(BF16)
    copies[2].wait()
    kt = dot(blended, wk[...], 1, 0).T.astype(BF16)
    copies[3].wait()
    vt = dot(wvt[...], blended, 1, 1).astype(BF16)
    for n in range(kv_out.shape[0]):
        kv_out[n, :DH] = kt
        kv_out[n, DH:] = vt


def lanes(ref, first, last):
    return jnp.concatenate([ref[n, first:last] for n in range(ref.shape[0])], axis=1)


SCALE = 1.0 / math.sqrt(DH)


def statistics(ins, outs):
    kv, ins = ins[0], ins[1:]
    blocks = len(ins) // 2
    q, do = ins[:blocks], ins[blocks:]
    (stats,) = outs
    k_rows = lanes(kv, 0, DH).T
    v_rows = lanes(kv, DH, DH + DV).T
    width = q[0].shape[1]
    for m in range(blocks):
        s = dot(k_rows, q[m][...], 1, 0) * SCALE
        top = jnp.max(s, axis=0, keepdims=True)
        e = jnp.exp(s - top)
        total = jnp.sum(e, axis=0, keepdims=True)
        dp = dot(v_rows, do[m][...], 1, 0)
        weighted = jnp.sum(e * dp, axis=0, keepdims=True)
        part = jnp.concatenate([top, total, weighted, jnp.zeros((5, width), F32)], axis=0)
        stats[:, m * width : (m + 1) * width] = part


def attend(ins, outs):
    kv, ins = ins[0], ins[1:]
    blocks = len(ins) // 3
    q, do, stats = ins[:blocks], ins[blocks : 2 * blocks], ins[2 * blocks :]
    odq, dkv = outs[:-1], outs[-1]
    kt = lanes(kv, 0, DH)
    vt = lanes(kv, DH, DH + DV)
    k_rows = kt.T
    v_rows = vt.T
    width = q[0].shape[1]
    dk = dv = None
    for m in range(blocks):
        part = [stats[c][:, (m ^ c) * width : ((m ^ c) + 1) * width] for c in range(blocks)]
        top = part[0][0:1]
        for x in part[1:]:
            top = jnp.maximum(top, x[0:1])
        total = jnp.zeros_like(top)
        weighted = jnp.zeros_like(top)
        for x in part:
            factor = jnp.exp(x[0:1] - top)
            total = total + factor * x[1:2]
            weighted = weighted + factor * x[2:3]
        row_dots = weighted / total
        s = dot(k_rows, q[m][...], 1, 0) * SCALE
        a = jnp.exp(s - top) / total
        ab = a.astype(BF16)
        dp = dot(v_rows, do[m][...], 1, 0)
        ds = (a * (dp - row_dots) * SCALE).astype(BF16)
        odq[m][:DV] = dot(vt, ab, 1, 0).astype(BF16)
        odq[m][DV:] = dot(kt, ds, 1, 0).astype(BF16)
        dk_m = dot(q[m][...], ds, 1, 1)
        dv_m = dot(do[m][...], ab, 1, 1)
        dk = dk_m if dk is None else dk + dk_m
        dv = dv_m if dv is None else dv + dv_m
    for n in range(dkv.shape[0]):
        dkv[n, :DH] = dk[:, n * width : (n + 1) * width].astype(BF16)
        dkv[n, DH:] = dv[:, n * width : (n + 1) * width].astype(BF16)


def add_up(pieces):
    total = pieces[0][...].astype(F32)
    for x in pieces[1:]:
        total = total + x[...].astype(F32)
    return total


def planes(ref):
    return [ref.at[n] for n in range(ref.shape[0])]


def features(ins, outs):
    dkv, wq, wk, wv = ins[:4]
    odq = ins[4:]
    attended, grads, feature = outs
    first = add_up(odq)
    second = add_up(planes(dkv)).astype(BF16)
    attended[...] = first[:DV].astype(BF16)
    dq = first[DV:].astype(BF16)
    grads[:DH] = dq
    grads[DH:] = second
    total = dot(wq[...], dq, 1, 0) + dot(wk[...], second[:DH], 1, 0)
    total = total + dot(wv[...], second[DH:], 1, 0)
    feature[...] = total.astype(BF16)


def outer(ins, outs):
    count = len(ins) // 2
    left, right = ins[:count], ins[count:]
    total = dot(left[0][...], right[0][...], 1, 1)
    for n in range(1, count):
        total = total + dot(left[n][...], right[n][...], 1, 1)
    outs[0][...] = total.astype(BF16)


def weight_sum(ins, outs, scale):
    total = add_up(planes(ins[0])) * scale
    rows = outs[0].shape[0]
    outs[0][...] = total[:rows, :DH]
    outs[1][...] = total[:rows, DH : 2 * DH]
    outs[2][...] = total[:rows, 2 * DH :]


def feature_sum(ins, outs):
    outs[0][...] = add_up(planes(ins[0])).astype(BF16)


def spread(ins, outs):
    own, low, high, taps = ins
    width = own.shape[1]
    body = own[...].astype(F32)
    padded = jnp.concatenate([low[...].astype(F32), body, high[...].astype(F32)], axis=1)
    summed = body
    for t in range(5):
        start = width - (t - 2) * DILATION_STEP
        summed = summed + taps[:, t : t + 1] * padded[:, start : start + width]
    outs[0][...] = summed


def local(tokens, conv_taps, w_query, w_key, w_value, grad_out):
    x = tokens[0]
    rows, columns = x.shape
    q_count = lax.axis_size(QGROUP)
    k_count = lax.axis_size(KGROUP)
    pair_count = lax.axis_size(PAIR)
    bx, core, sx = (lax.axis_size(a) for a in ("bx", "core", "sx"))
    y = lax.axis_size(("yh", "yl"))
    rest = bx * y
    share = columns // (bx * core * sx * y)
    heads = lax.axis_size("heads")
    slice_width = columns // heads

    do = gather(grad_out[0].T, QGROUP)
    low, high = shift_pair(x[rows - REACH :], x[:REACH], SEQ)
    low, high, *do = lax.optimization_barrier((low, high, *do))
    blended, qt, kv_all = call(
        project,
        [((rows, columns), BF16), ((DH, rows), BF16), ((k_count, DH + DV, rows), BF16)],
        x, w_query, w_key, w_value.T, low, high, conv_taps,
        far=4, vmem=62 << 20,
    )
    kv = exchange(kv_all, KGROUP)
    q = gather(qt, QGROUP)

    groups = blended.reshape(rows, bx, core, sx, y, share)
    groups = jnp.pad(groups, ((0, 0),) * 5 + ((0, PAD - share),))
    groups = groups.transpose(2, 3, 1, 4, 5, 0).reshape(pair_count, rest * PAD, rows)
    mine = lax.axis_index(PAIR)
    left = trade(
        [lax.dynamic_index_in_dim(groups, mine ^ k, 0, False) for k in range(pair_count)], PAIR
    )

    (stats,) = call(statistics, [((8, q_count * rows), F32)], kv, *q, *do)
    stats = gather(stats, QGROUP)
    *odq, dkv = call(
        attend,
        [((DH + DV, rows), BF16)] * q_count + [((k_count, DH + DV, rows), BF16)],
        kv, *q, *do, *stats,
    )
    dkv = exchange(dkv, KGROUP)
    odq = trade(odq, QGROUP)
    dkv, *left = lax.optimization_barrier((dkv, *left))
    attended, grads, feature = call(
        features,
        [((DV, rows), BF16), ((2 * DH + DV, rows), BF16), ((columns, rows), BF16)],
        dkv, w_query, w_key, w_value, *odq,
    )
    right = gather(grads, PAIR)
    feature = exchange(feature.reshape(heads, slice_width, rows), "heads")
    (product,) = call(outer, [((rest * PAD, 2 * DH + DV), BF16)], *left, *right)
    product = exchange(product.reshape(rest, PAD, 2 * DH + DV), REST)

    (own,) = call(feature_sum, [((slice_width, rows), BF16)], feature)
    before, after = shift_pair(own, own, SEQ)
    taps = lax.dynamic_slice_in_dim(
        conv_taps, lax.axis_index("heads") * slice_width, slice_width, 1
    ).T
    (grad_tokens,) = call(spread, [((slice_width, rows), F32)], own, before, after, taps)
    scale = 1.0 / math.sqrt(bx * core * sx * y * rows)
    grad_query, grad_key, grad_value = call(
        lambda i, o: weight_sum(i, o, scale),
        [((share, DH), F32), ((share, DH), F32), ((share, DV), F32)],
        product,
    )
    return attended.T[None], grad_tokens.T[None], grad_query, grad_key, grad_value


def split(mesh):
    batch, heads, seq = mesh.devices.shape
    shape = (batch // 2, 2, heads, 2, seq // 4, 2)
    return Mesh(mesh.devices.reshape(shape), ("bx", "core", "heads", "sx", "yh", "yl"))


def solution(mesh):
    batch = ("bx", "core")
    whole = split(mesh)
    return jax.shard_map(
        local,
        mesh=whole,
        in_specs=(
            P(batch, SEQ, None),
            P(),
            P(None, "heads"),
            P(None, "heads"),
            P(None, "heads"),
            P(batch, SEQ, "heads"),
        ),
        out_specs=(
            P(batch, SEQ, "heads"),
            P(batch, SEQ, "heads"),
            P(batch + SEQ, "heads"),
            P(batch + SEQ, "heads"),
            P(batch + SEQ, "heads"),
        ),
        check_vma=False,
    )
```

```python
import math

import jax
import jax.numpy as jnp
from jax import lax
from jax.experimental import pallas as pl
from jax.experimental.pallas import tpu as pltpu
from jax.sharding import Mesh
from jax.sharding import PartitionSpec as P

DH = 128
DV = 192
DILATION_STEP = 4
REACH = 2 * DILATION_STEP
PAD = 16
VMEM = 16 << 20

F32 = jnp.float32
BF16 = jnp.bfloat16
SEQ = ("sx", "y")
QGROUP = "sx"
KGROUP = "y"
REST = ("bx", "y")


def dot(a, b, ca, cb):
    return lax.dot_general(a, b, (((ca,), (cb,)), ((), ())), preferred_element_type=F32)


def call(body, outs, *args, name):
    def kernel(*refs):
        body(refs[: len(args)], refs[len(args) :])

    return pl.pallas_call(
        kernel,
        out_shape=[jax.ShapeDtypeStruct(s, t) for s, t in outs],
        name=name,
        compiler_params=pltpu.CompilerParams(vmem_limit_bytes=VMEM),
    )(*args)


def exchange(x, axis):
    return lax.all_to_all(x, axis, split_axis=0, concat_axis=0, tiled=True)


def swap(x, axis):
    return lax.ppermute(x, axis, [(0, 1), (1, 0)])


def shift_pair(low_source, high_source, axes):
    count = lax.axis_size(axes)
    forward = [(i, i + 1) for i in range(count - 1)]
    backward = [(j, i) for i, j in forward]
    return lax.ppermute(low_source, axes, forward), lax.ppermute(high_source, axes, backward)


def blend(ins, outs):
    tokens, taps = ins
    rows, columns = tokens.shape
    body = tokens[...].astype(F32)
    edge = jnp.zeros((REACH, columns), F32)
    padded = jnp.concatenate([edge, body, edge], axis=0)
    summed = body
    for t in range(5):
        summed = summed + taps[t : t + 1, :] * padded[t * DILATION_STEP : t * DILATION_STEP + rows]
    outs[0][...] = summed


def project(ins, outs):
    inner, low, high, taps, weights, do = ins
    blended_out, qdo, kv_out = outs
    rows, columns = inner.shape
    low = low[...].astype(F32)
    high = high[...].astype(F32)
    none = jnp.zeros((DILATION_STEP, columns), F32)
    first = taps[0:1] * low + jnp.concatenate([taps[1:2] * low[DILATION_STEP:], none], axis=0)
    last = taps[4:5] * high + jnp.concatenate([none, taps[3:4] * high[:DILATION_STEP]], axis=0)
    summed = jnp.concatenate(
        [inner[:REACH] + first, inner[REACH : rows - REACH], inner[rows - REACH :] + last], axis=0
    )
    blended = summed.astype(BF16)
    blended_out[...] = blended
    qkv = dot(blended, weights[...], 1, 0).T.astype(BF16)
    qdo[:DH] = qkv[:DH]
    qdo[DH:] = do[...]
    for n in range(kv_out.shape[0]):
        kv_out[n] = qkv[DH:]


def lanes(ref, first, last):
    return jnp.concatenate([ref[n, first:last] for n in range(ref.shape[0])], axis=1)


SCALE = 1.0 / math.sqrt(DH)


def statistics(ins, outs):
    kv, qdos = ins[0], ins[1:]
    (stats,) = outs
    k_rows = lanes(kv, 0, DH).T
    v_rows = lanes(kv, DH, DH + DV).T
    width = qdos[0].shape[1]
    for m, qdo in enumerate(qdos):
        s = dot(k_rows, qdo[:DH], 1, 0) * SCALE
        top = jnp.max(s, axis=0, keepdims=True)
        e = jnp.exp(s - top)
        total = jnp.sum(e, axis=0, keepdims=True)
        dp = dot(v_rows, qdo[DH:], 1, 0)
        weighted = jnp.sum(e * dp, axis=0, keepdims=True)
        part = jnp.concatenate([top, total, weighted, jnp.zeros((5, width), F32)], axis=0)
        stats[:, m * width : (m + 1) * width] = part


def attend(ins, outs):
    kv, ins = ins[0], ins[1:]
    blocks = len(ins) // 2
    qdos, stats = ins[:blocks], ins[blocks:]
    odq, dkv = outs[:-1], outs[-1]
    kt = lanes(kv, 0, DH)
    vt = lanes(kv, DH, DH + DV)
    k_rows = kt.T
    v_rows = vt.T
    width = qdos[0].shape[1]
    dk = dv = None
    for m, qdo in enumerate(qdos):
        part = [stats[c][:, (m ^ c) * width : ((m ^ c) + 1) * width] for c in range(blocks)]
        top = part[0][0:1]
        for x in part[1:]:
            top = jnp.maximum(top, x[0:1])
        total = jnp.zeros_like(top)
        weighted = jnp.zeros_like(top)
        for x in part:
            factor = jnp.exp(x[0:1] - top)
            total = total + factor * x[1:2]
            weighted = weighted + factor * x[2:3]
        row_dots = weighted / total
        s = dot(k_rows, qdo[:DH], 1, 0) * SCALE
        a = jnp.exp(s - top) / total
        ab = a.astype(BF16)
        dp = dot(v_rows, qdo[DH:], 1, 0)
        ds = (a * (dp - row_dots) * SCALE).astype(BF16)
        odq[m][:DV] = dot(vt, ab, 1, 0).astype(BF16)
        odq[m][DV:] = dot(kt, ds, 1, 0).astype(BF16)
        dk_m = dot(qdo[:DH], ds, 1, 1)
        dv_m = dot(qdo[DH:], ab, 1, 1)
        dk = dk_m if dk is None else dk + dk_m
        dv = dv_m if dv is None else dv + dv_m
    for n in range(dkv.shape[0]):
        dkv[n, :DH] = dk[:, n * width : (n + 1) * width].astype(BF16)
        dkv[n, DH:] = dv[:, n * width : (n + 1) * width].astype(BF16)


def add_up(pieces):
    total = pieces[0][...].astype(F32)
    for x in pieces[1:]:
        total = total + x[...].astype(F32)
    return total


def planes(ref):
    return [ref.at[n] for n in range(ref.shape[0])]


def features(ins, outs):
    dkv, weights = ins[:2]
    odq = ins[2:]
    attended, grads, feature = outs
    first = add_up(odq)
    second = add_up(planes(dkv)).astype(BF16)
    attended[...] = first[:DV].astype(BF16)
    all_grads = jnp.concatenate([first[DV:].astype(BF16), second], axis=0)
    grads[...] = all_grads
    feature[...] = dot(weights[...], all_grads, 1, 0).astype(BF16)


def outer(ins, outs):
    own, near, far, grads, near_grads, far_grads = ins
    pairs = [(own[...], grads[...]), (near[...], near_grads[...])]
    pairs += [(far[n], far_grads[n]) for n in range(far.shape[0])]
    total = None
    for left, right in pairs:
        term = dot(left, right, 1, 1)
        total = term if total is None else total + term
    outs[0][...] = total.astype(BF16)


def weight_sum(ins, outs, scale):
    total = add_up(planes(ins[0])) * scale
    rows = outs[0].shape[0]
    outs[0][...] = total[:rows, :DH]
    outs[1][...] = total[:rows, DH : 2 * DH]
    outs[2][...] = total[:rows, 2 * DH :]


def feature_sum(ins, outs):
    outs[0][...] = add_up(planes(ins[0])).astype(BF16)


def spread(ins, outs):
    own, low, high, taps = ins
    width = own.shape[1]
    body = own[...].astype(F32)
    padded = jnp.concatenate([low[...].astype(F32), body, high[...].astype(F32)], axis=1)
    summed = body
    for t in range(5):
        start = width - (t - 2) * DILATION_STEP
        summed = summed + taps[:, t : t + 1] * padded[:, start : start + width]
    outs[0][...] = summed


def local(tokens, conv_taps, w_query, w_key, w_value, grad_out):
    x = tokens[0]
    rows, columns = x.shape
    k_count = lax.axis_size(KGROUP)
    bx, core, sx, y = (lax.axis_size(a) for a in ("bx", "core", "sx", "y"))
    rest = bx * y
    share = columns // (bx * core * sx * y)
    heads = lax.axis_size("heads")
    slice_width = columns // heads
    width = 2 * DH + DV

    low, high = shift_pair(x[rows - REACH :], x[:REACH], SEQ)
    weights = jnp.concatenate([w_query, w_key, w_value], axis=1)
    (inner,) = call(blend, [((rows, columns), F32)], x, conv_taps, name="blend")
    blended, qdo, kv_all = call(
        project,
        [((rows, columns), BF16), ((DH + DV, rows), BF16), ((k_count, DH + DV, rows), BF16)],
        inner, low, high, conv_taps, weights, grad_out[0].T,
        name="project",
    )
    kv = exchange(kv_all, KGROUP)
    qdos = [qdo, swap(qdo, QGROUP)]

    groups = blended.reshape(rows, bx, core, sx, y, share)
    groups = jnp.pad(groups, ((0, 0),) * 5 + ((0, PAD - share),))
    groups = groups.transpose(2, 3, 1, 4, 5, 0).reshape(core, sx, rest * PAD, rows)
    mine = lax.axis_index("core")
    side = lax.axis_index("sx")
    kept = lax.dynamic_index_in_dim(groups, mine, 0, False)
    got = swap(lax.dynamic_index_in_dim(groups, 1 - mine, 0, False), "core")
    own = lax.dynamic_index_in_dim(kept, side, 0, False)
    near = lax.dynamic_index_in_dim(got, side, 0, False)
    far = swap(
        jnp.stack(
            [
                lax.dynamic_index_in_dim(kept, 1 - side, 0, False),
                lax.dynamic_index_in_dim(got, 1 - side, 0, False),
            ]
        ),
        "sx",
    )
    kv, own, near, far = lax.optimization_barrier((kv, own, near, far))

    (stats,) = call(statistics, [((8, sx * rows), F32)], kv, *qdos, name="statistics")
    *odq, dkv = call(
        attend,
        [((DH + DV, rows), BF16)] * sx + [((k_count, DH + DV, rows), BF16)],
        kv, *qdos, stats, swap(stats, QGROUP),
        name="attend",
    )
    dkv = exchange(dkv, KGROUP)
    attended, grads, feature = call(
        features,
        [((DV, rows), BF16), ((width, rows), BF16), ((columns, rows), BF16)],
        dkv, weights, odq[0], swap(odq[1], QGROUP),
        name="features",
    )
    near_grads = swap(grads, "core")
    far_grads = swap(jnp.stack([grads, near_grads]), "sx")
    feature = exchange(feature.reshape(heads, slice_width, rows), "heads")
    (product,) = call(
        outer, [((rest * PAD, width), BF16)],
        own, near, far, grads, near_grads, far_grads,
        name="outer",
    )
    product = exchange(product.reshape(rest, PAD, width), REST)

    (own,) = call(feature_sum, [((slice_width, rows), BF16)], feature, name="feature_sum")
    before, after = shift_pair(own, own, SEQ)
    taps = lax.dynamic_slice_in_dim(
        conv_taps, lax.axis_index("heads") * slice_width, slice_width, 1
    ).T
    (grad_tokens,) = call(
        spread, [((slice_width, rows), F32)], own, before, after, taps, name="spread"
    )
    scale = 1.0 / math.sqrt(bx * core * sx * y * rows)
    grad_query, grad_key, grad_value = call(
        lambda i, o: weight_sum(i, o, scale),
        [((share, DH), F32), ((share, DH), F32), ((share, DV), F32)],
        product,
        name="weight_sum",
    )
    return attended.T[None], grad_tokens.T[None], grad_query, grad_key, grad_value


def split(mesh):
    batch, heads, seq = mesh.devices.shape
    shape = (batch // 2, 2, heads, 2, seq // 2)
    return Mesh(mesh.devices.reshape(shape), ("bx", "core", "heads", "sx", "y"))


def solution(mesh):
    batch = ("bx", "core")
    whole = split(mesh)
    return jax.shard_map(
        local,
        mesh=whole,
        in_specs=(
            P(batch, SEQ, None),
            P(),
            P(None, "heads"),
            P(None, "heads"),
            P(None, "heads"),
            P(batch, SEQ, "heads"),
        ),
        out_specs=(
            P(batch, SEQ, "heads"),
            P(batch, SEQ, "heads"),
            P(batch + SEQ, "heads"),
            P(batch + SEQ, "heads"),
            P(batch + SEQ, "heads"),
        ),
        check_vma=False,
    )
```

```python
import math

import jax
import jax.numpy as jnp
from jax import lax
from jax.experimental import pallas as pl
from jax.experimental.pallas import tpu as pltpu
from jax.sharding import Mesh
from jax.sharding import PartitionSpec as P

DH = 128
DV = 192
DILATION_STEP = 4
REACH = 2 * DILATION_STEP
PAD = 16
SHARE = 12
FOLD = 3
VMEM = 16 << 20

F32 = jnp.float32
BF16 = jnp.bfloat16
SEQ = ("sx", "y")
QGROUP = "sx"
KGROUP = "y"
REST = ("bx", "y")


def dot(a, b, ca, cb):
    return lax.dot_general(a, b, (((ca,), (cb,)), ((), ())), preferred_element_type=F32)


def call(body, outs, *args, name):
    def kernel(*refs):
        body(refs[: len(args)], refs[len(args) :])

    return pl.pallas_call(
        kernel,
        out_shape=[jax.ShapeDtypeStruct(s, t) for s, t in outs],
        name=name,
        compiler_params=pltpu.CompilerParams(vmem_limit_bytes=VMEM),
    )(*args)


def exchange(x, axis):
    return lax.all_to_all(x, axis, split_axis=0, concat_axis=0, tiled=True)


def swap(x, axis):
    return lax.ppermute(x, axis, [(0, 1), (1, 0)])


def shift_pair(low_source, high_source, axes):
    count = lax.axis_size(axes)
    forward = [(i, i + 1) for i in range(count - 1)]
    backward = [(j, i) for i, j in forward]
    return lax.ppermute(low_source, axes, forward), lax.ppermute(high_source, axes, backward)


def blend(ins, outs):
    tokens, taps = ins
    rows, columns = tokens.shape
    body = tokens[...].astype(F32)
    edge = jnp.zeros((REACH, columns), F32)
    padded = jnp.concatenate([edge, body, edge], axis=0)
    summed = body
    for t in range(5):
        summed = summed + taps[t : t + 1, :] * padded[t * DILATION_STEP : t * DILATION_STEP + rows]
    outs[0][...] = summed


def project(ins, outs):
    inner, low, high, taps, weights, do = ins
    blended_out, qdo, kv_out = outs
    rows, columns = inner.shape
    low = low[...].astype(F32)
    high = high[...].astype(F32)
    none = jnp.zeros((DILATION_STEP, columns), F32)
    first = taps[0:1] * low + jnp.concatenate([taps[1:2] * low[DILATION_STEP:], none], axis=0)
    last = taps[4:5] * high + jnp.concatenate([none, taps[3:4] * high[:DILATION_STEP]], axis=0)
    summed = jnp.concatenate(
        [inner[:REACH] + first, inner[REACH : rows - REACH], inner[rows - REACH :] + last], axis=0
    )
    blended = summed.astype(BF16)
    blended_out[...] = blended
    qkv = dot(blended, weights[...], 1, 0).T.astype(BF16)
    qdo[:DH] = qkv[:DH]
    qdo[DH:] = do[...]
    for n in range(kv_out.shape[0]):
        kv_out[n] = qkv[DH:]


def lanes(ref, first, last):
    return jnp.concatenate([ref[n, first:last] for n in range(ref.shape[0])], axis=1)


SCALE = 1.0 / math.sqrt(DH)


def statistics(ins, outs):
    kv, qdos = ins[0], ins[1:]
    (stats,) = outs
    k_rows = lanes(kv, 0, DH).T
    v_rows = lanes(kv, DH, DH + DV).T
    width = qdos[0].shape[1]
    for m, qdo in enumerate(qdos):
        s = dot(k_rows, qdo[:DH], 1, 0) * SCALE
        top = jnp.max(s, axis=0, keepdims=True)
        e = jnp.exp(s - top)
        total = jnp.sum(e, axis=0, keepdims=True)
        dp = dot(v_rows, qdo[DH:], 1, 0)
        weighted = jnp.sum(e * dp, axis=0, keepdims=True)
        part = jnp.concatenate([top, total, weighted, jnp.zeros((5, width), F32)], axis=0)
        stats[:, m * width : (m + 1) * width] = part


def attend(ins, outs):
    kv, ins = ins[0], ins[1:]
    blocks = len(ins) // 2
    qdos, stats = ins[:blocks], ins[blocks:]
    odq, dkv = outs[:-1], outs[-1]
    kt = lanes(kv, 0, DH)
    vt = lanes(kv, DH, DH + DV)
    k_rows = kt.T
    v_rows = vt.T
    width = qdos[0].shape[1]
    dk = dv = None
    for m, qdo in enumerate(qdos):
        part = [stats[c][:, (m ^ c) * width : ((m ^ c) + 1) * width] for c in range(blocks)]
        top = part[0][0:1]
        for x in part[1:]:
            top = jnp.maximum(top, x[0:1])
        total = jnp.zeros_like(top)
        weighted = jnp.zeros_like(top)
        for x in part:
            factor = jnp.exp(x[0:1] - top)
            total = total + factor * x[1:2]
            weighted = weighted + factor * x[2:3]
        row_dots = weighted / total
        s = dot(k_rows, qdo[:DH], 1, 0) * SCALE
        a = jnp.exp(s - top) / total
        ab = a.astype(BF16)
        dp = dot(v_rows, qdo[DH:], 1, 0)
        ds = (a * (dp - row_dots) * SCALE).astype(BF16)
        odq[m][:DV] = dot(vt, ab, 1, 0).astype(BF16)
        odq[m][DV:] = dot(kt, ds, 1, 0).astype(BF16)
        dk_m = dot(qdo[:DH], ds, 1, 1)
        dv_m = dot(qdo[DH:], ab, 1, 1)
        dk = dk_m if dk is None else dk + dk_m
        dv = dv_m if dv is None else dv + dv_m
    for n in range(dkv.shape[0]):
        dkv[n, :DH] = dk[:, n * width : (n + 1) * width].astype(BF16)
        dkv[n, DH:] = dv[:, n * width : (n + 1) * width].astype(BF16)


def add_up(pieces):
    total = pieces[0][...].astype(F32)
    for x in pieces[1:]:
        total = total + x[...].astype(F32)
    return total


def planes(ref):
    return [ref.at[n] for n in range(ref.shape[0])]


def features(ins, outs):
    dkv, weights = ins[:2]
    odq = ins[2:]
    attended, grads, feature = outs
    first = add_up(odq)
    second = add_up(planes(dkv)).astype(BF16)
    attended[...] = first[:DV].astype(BF16)
    all_grads = jnp.concatenate([first[DV:].astype(BF16), second], axis=0)
    grads[...] = all_grads
    feature[...] = dot(weights[...], all_grads, 1, 0).astype(BF16)


def outer(ins, outs):
    own, near, far, grads, far_grads, near_grads = ins
    pairs = [
        (own[...], grads[...]),
        (near[...], near_grads[0]),
        (far[0], far_grads[...]),
        (far[1], near_grads[1]),
    ]
    total = None
    for left, right in pairs:
        term = dot(left, right, 1, 1)
        total = term if total is None else total + term
    main = outs[0].shape[1]
    span = total.shape[1] - main
    block = 128
    row = lax.broadcasted_iota(jnp.int32, (block, block), 0)
    column = lax.broadcasted_iota(jnp.int32, (block, block), 1)
    spare = (row & (PAD - 1)) - SHARE
    source = row - (row & (PAD - 1)) + FOLD * spare
    picks = [
        jnp.where((spare >= 0) & (column == source + b), 1.0, 0.0).astype(BF16)
        for b in range(FOLD)
    ]
    tail = total[:, main:].astype(BF16)
    blank = jnp.zeros((block, span), F32)
    for n in range(total.shape[0] // block):
        rows = slice(n * block, (n + 1) * block)
        moved = [dot(e, tail[rows], 1, 0) for e in picks] + [blank]
        for c in range(2):
            lane = slice(c * DH, (c + 1) * DH)
            extra = jnp.concatenate(moved[2 * c : 2 * c + 2], axis=1)
            outs[0][rows, lane] = (total[rows, lane] + extra).astype(BF16)
        outs[0][rows, 2 * DH :] = total[rows, 2 * DH : main].astype(BF16)


def weight_sum(ins, outs, scale):
    total = add_up(planes(ins[0])) * scale
    span = 2 * DH + DV - total.shape[1]
    outs[0][...] = total[:SHARE, :DH]
    outs[1][...] = total[:SHARE, DH : 2 * DH]
    outs[2][:, : DV - span] = total[:SHARE, 2 * DH :]
    for r in range(SHARE):
        a, b = SHARE + r // FOLD, r % FOLD
        outs[2][r : r + 1, DV - span :] = total[a : a + 1, b * span : (b + 1) * span]


def feature_sum(ins, outs):
    outs[0][...] = add_up(planes(ins[0])).astype(BF16)


def spread(ins, outs):
    own, low, high, taps = ins
    width = own.shape[1]
    body = own[...].astype(F32)
    padded = jnp.concatenate([low[...].astype(F32), body, high[...].astype(F32)], axis=1)
    summed = body
    for t in range(5):
        start = width - (t - 2) * DILATION_STEP
        summed = summed + taps[:, t : t + 1] * padded[:, start : start + width]
    outs[0][...] = summed


def local(tokens, conv_taps, w_query, w_key, w_value, grad_out):
    x = tokens[0]
    rows, columns = x.shape
    k_count = lax.axis_size(KGROUP)
    bx, core, sx, y = (lax.axis_size(a) for a in ("bx", "core", "sx", "y"))
    rest = bx * y
    share = columns // (bx * core * sx * y)
    heads = lax.axis_size("heads")
    slice_width = columns // heads
    width = 2 * DH + DV
    packed = width - DV % DH

    low, high = shift_pair(x[rows - REACH :], x[:REACH], SEQ)
    weights = jnp.concatenate([w_query, w_key, w_value], axis=1)
    (inner,) = call(blend, [((rows, columns), F32)], x, conv_taps, name="blend")
    blended, qdo, kv_all = call(
        project,
        [((rows, columns), BF16), ((DH + DV, rows), BF16), ((k_count, DH + DV, rows), BF16)],
        inner, low, high, conv_taps, weights, grad_out[0].T,
        name="project",
    )
    kv = exchange(kv_all, KGROUP)
    qdos = [qdo, swap(qdo, QGROUP)]

    groups = blended.reshape(rows, bx, core, sx, y, share)
    groups = jnp.pad(groups, ((0, 0),) * 5 + ((0, PAD - share),))
    groups = groups.transpose(2, 3, 1, 4, 5, 0).reshape(core, sx, rest * PAD, rows)
    mine = lax.axis_index("core")
    side = lax.axis_index("sx")
    kept = lax.dynamic_index_in_dim(groups, mine, 0, False)
    got = swap(lax.dynamic_index_in_dim(groups, 1 - mine, 0, False), "core")
    own = lax.dynamic_index_in_dim(kept, side, 0, False)
    near = lax.dynamic_index_in_dim(got, side, 0, False)
    crossing = jnp.stack(
        [
            lax.dynamic_index_in_dim(kept, 1 - side, 0, False),
            lax.dynamic_index_in_dim(got, 1 - side, 0, False),
        ]
    )
    kv, own, near, crossing = lax.optimization_barrier((kv, own, near, crossing))

    (stats,) = call(statistics, [((8, sx * rows), F32)], kv, *qdos, name="statistics")
    *odq, dkv = call(
        attend,
        [((DH + DV, rows), BF16)] * sx + [((k_count, DH + DV, rows), BF16)],
        kv, *qdos, stats, swap(stats, QGROUP),
        name="attend",
    )
    dkv, far = lax.optimization_barrier((exchange(dkv, KGROUP), swap(crossing, "sx")))
    attended, grads, feature = call(
        features,
        [((DV, rows), BF16), ((width, rows), BF16), ((columns, rows), BF16)],
        dkv, weights, odq[0], swap(odq[1], QGROUP),
        name="features",
    )
    far_grads = swap(grads, "sx")
    near_grads = swap(jnp.stack([grads, far_grads]), "core")
    feature = exchange(feature.reshape(heads, slice_width, rows), "heads")
    (product,) = call(
        outer, [((rest * PAD, packed), BF16)],
        own, near, far, grads, far_grads, near_grads,
        name="outer",
    )
    product = exchange(product.reshape(rest, PAD, packed), REST)

    (own,) = call(feature_sum, [((slice_width, rows), BF16)], feature, name="feature_sum")
    before, after = shift_pair(own, own, SEQ)
    taps = lax.dynamic_slice_in_dim(
        conv_taps, lax.axis_index("heads") * slice_width, slice_width, 1
    ).T
    (grad_tokens,) = call(
        spread, [((slice_width, rows), F32)], own, before, after, taps, name="spread"
    )
    scale = 1.0 / math.sqrt(bx * core * sx * y * rows)
    grad_query, grad_key, grad_value = call(
        lambda i, o: weight_sum(i, o, scale),
        [((share, DH), F32), ((share, DH), F32), ((share, DV), F32)],
        product,
        name="weight_sum",
    )
    return attended.T[None], grad_tokens.T[None], grad_query, grad_key, grad_value


def split(mesh):
    batch, heads, seq = mesh.devices.shape
    shape = (batch // 2, 2, heads, 2, seq // 2)
    return Mesh(mesh.devices.reshape(shape), ("bx", "core", "heads", "sx", "y"))


def solution(mesh):
    batch = ("bx", "core")
    whole = split(mesh)
    return jax.shard_map(
        local,
        mesh=whole,
        in_specs=(
            P(batch, SEQ, None),
            P(),
            P(None, "heads"),
            P(None, "heads"),
            P(None, "heads"),
            P(batch, SEQ, "heads"),
        ),
        out_specs=(
            P(batch, SEQ, "heads"),
            P(batch, SEQ, "heads"),
            P(batch + SEQ, "heads"),
            P(batch + SEQ, "heads"),
            P(batch + SEQ, "heads"),
        ),
        check_vma=False,
    )
```

```python
import math

import jax
import jax.numpy as jnp
from jax import lax
from jax.experimental import pallas as pl
from jax.experimental.pallas import tpu as pltpu
from jax.sharding import Mesh
from jax.sharding import PartitionSpec as P

DH = 128
DV = 192
DILATION_STEP = 4
REACH = 2 * DILATION_STEP
PAD = 16
SHARE = 12
FOLD = 3
VMEM = 16 << 20

F32 = jnp.float32
BF16 = jnp.bfloat16
SEQ = ("sx", "y")
QGROUP = "sx"
KGROUP = "y"
REST = ("bx", "y")


def dot(a, b, ca, cb):
    return lax.dot_general(a, b, (((ca,), (cb,)), ((), ())), preferred_element_type=F32)


def call(body, outs, *args, name, staged=None):
    count = len(args)

    def kernel(*refs):
        ins, results = refs[:count], refs[count : count + len(outs)]
        if staged is None:
            body(ins, results)
            return
        held, sems = refs[-2], refs[-1]
        target = results[-1]
        copies = []

        def ship(source, place):
            if copies:
                copies[-1].start()
            copies.append(
                pltpu.make_async_copy(source, target.at[place], sems.at[len(copies)])
            )

        body(ins, results[:-1], held, ship)
        copies[-1].start()
        for copy in copies:
            copy.wait()

    near = pl.BlockSpec(memory_space=pltpu.VMEM)
    specs = [near] * len(outs)
    scratch = []
    if staged is not None:
        shape, pieces = staged
        specs[-1] = pl.BlockSpec(memory_space=pl.ANY)
        scratch = [pltpu.VMEM(shape, outs[-1][1]), pltpu.SemaphoreType.DMA((pieces,))]
    return pl.pallas_call(
        kernel,
        out_shape=[jax.ShapeDtypeStruct(s, t) for s, t in outs],
        in_specs=[near] * count,
        out_specs=specs,
        scratch_shapes=scratch,
        name=name,
        compiler_params=pltpu.CompilerParams(vmem_limit_bytes=VMEM),
    )(*args)


def exchange(x, axis):
    return lax.all_to_all(x, axis, split_axis=0, concat_axis=0, tiled=True)


def swap(x, axis):
    return lax.ppermute(x, axis, [(0, 1), (1, 0)])


def shift_pair(low_source, high_source, axes):
    count = lax.axis_size(axes)
    forward = [(i, i + 1) for i in range(count - 1)]
    backward = [(j, i) for i, j in forward]
    return lax.ppermute(low_source, axes, forward), lax.ppermute(high_source, axes, backward)


def blend(ins, outs):
    tokens, taps = ins
    rows, columns = tokens.shape
    body = tokens[...].astype(F32)
    edge = jnp.zeros((REACH, columns), F32)
    padded = jnp.concatenate([edge, body, edge], axis=0)
    summed = body
    for t in range(5):
        summed = summed + taps[t : t + 1, :] * padded[t * DILATION_STEP : t * DILATION_STEP + rows]
    outs[0][...] = summed


def project(ins, outs, held, ship, copies):
    inner, low, high, taps, weights, do = ins
    blended_out, qdo = outs
    rows, columns = inner.shape
    low = low[...].astype(F32)
    high = high[...].astype(F32)
    none = jnp.zeros((DILATION_STEP, columns), F32)
    first = taps[0:1] * low + jnp.concatenate([taps[1:2] * low[DILATION_STEP:], none], axis=0)
    last = taps[4:5] * high + jnp.concatenate([none, taps[3:4] * high[:DILATION_STEP]], axis=0)
    summed = jnp.concatenate(
        [inner[:REACH] + first, inner[REACH : rows - REACH], inner[rows - REACH :] + last], axis=0
    )
    blended = summed.astype(BF16)
    qkv = dot(blended, weights[...], 1, 0).T.astype(BF16)
    held[...] = qkv[DH:]
    qdo[:DH] = qkv[:DH]
    qdo[DH:] = do[...]
    for n in range(copies):
        ship(held, n)
    blended_out[...] = blended


def lanes(ref, first, last):
    return jnp.concatenate([ref[n, first:last] for n in range(ref.shape[0])], axis=1)


SCALE = 1.0 / math.sqrt(DH)


def statistics(ins, outs):
    kv, qdos = ins[0], ins[1:]
    stats, exponents, products = outs
    k_rows = lanes(kv, 0, DH).T
    v_rows = lanes(kv, DH, DH + DV).T
    width = qdos[0].shape[1]
    for m, qdo in enumerate(qdos):
        s = dot(k_rows, qdo[:DH], 1, 0) * SCALE
        top = jnp.max(s, axis=0, keepdims=True)
        e = jnp.exp(s - top)
        total = jnp.sum(e, axis=0, keepdims=True)
        dp = dot(v_rows, qdo[DH:], 1, 0)
        weighted = jnp.sum(e * dp, axis=0, keepdims=True)
        part = jnp.concatenate([top, total, weighted, jnp.zeros((5, width), F32)], axis=0)
        lane = slice(m * width, (m + 1) * width)
        stats[:, lane] = part
        exponents[:, lane] = e
        products[:, lane] = dp


def attend(ins, outs, dkv, ship):
    kv, exponents, products = ins[:3]
    blocks = len(outs)
    qdos, stats = ins[3 : 3 + blocks], ins[3 + blocks :]
    odq = outs
    kt = lanes(kv, 0, DH)
    vt = lanes(kv, DH, DH + DV)
    width = qdos[0].shape[1]
    dk = dv = None
    for m, qdo in enumerate(qdos):
        part = [stats[c][:, (m ^ c) * width : ((m ^ c) + 1) * width] for c in range(blocks)]
        top = part[0][0:1]
        for x in part[1:]:
            top = jnp.maximum(top, x[0:1])
        total = jnp.zeros_like(top)
        weighted = jnp.zeros_like(top)
        for x in part:
            factor = jnp.exp(x[0:1] - top)
            total = total + factor * x[1:2]
            weighted = weighted + factor * x[2:3]
        row_dots = weighted / total
        lane = slice(m * width, (m + 1) * width)
        a = exponents[:, lane] * (jnp.exp(part[0][0:1] - top) / total)
        ab = a.astype(BF16)
        ds = (a * (products[:, lane] - row_dots) * SCALE).astype(BF16)
        odq[m][:DV] = dot(vt, ab, 1, 0).astype(BF16)
        odq[m][DV:] = dot(kt, ds, 1, 0).astype(BF16)
        dk_m = dot(qdo[:DH], ds, 1, 1)
        dv_m = dot(qdo[DH:], ab, 1, 1)
        dk = dk_m if dk is None else dk + dk_m
        dv = dv_m if dv is None else dv + dv_m
    for n in range(dkv.shape[0]):
        dkv[n, :DH] = dk[:, n * width : (n + 1) * width].astype(BF16)
        dkv[n, DH:] = dv[:, n * width : (n + 1) * width].astype(BF16)
        ship(dkv.at[n], n)


def add_up(pieces):
    total = pieces[0][...].astype(F32)
    for x in pieces[1:]:
        total = total + x[...].astype(F32)
    return total


def planes(ref):
    return [ref.at[n] for n in range(ref.shape[0])]


def features(ins, outs, held, ship):
    dkv, weights = ins[:2]
    odq = ins[2:]
    attended, grads = outs
    first = add_up(odq)
    second = add_up(planes(dkv)).astype(BF16)
    all_grads = jnp.concatenate([first[DV:].astype(BF16), second], axis=0)
    size = held.shape[1]
    for n in range(held.shape[0]):
        rows = slice(n * size, (n + 1) * size)
        held[n] = dot(weights[rows], all_grads, 1, 0).astype(BF16)
        ship(held.at[n], n)
    grads[...] = all_grads
    attended[...] = first[:DV].astype(BF16)


def outer(ins, outs, held, ship):
    own, near, far, grads, far_grads, near_grads = ins
    pairs = [
        (own, grads[...]),
        (near, near_grads[0]),
        (far.at[0], far_grads[...]),
        (far.at[1], near_grads[1]),
    ]
    main = held.shape[1]
    span = grads.shape[0] - main
    block = 128
    row = lax.broadcasted_iota(jnp.int32, (block, block), 0)
    column = lax.broadcasted_iota(jnp.int32, (block, block), 1)
    spare = (row & (PAD - 1)) - SHARE
    source = row - (row & (PAD - 1)) + FOLD * spare
    picks = [
        jnp.where((spare >= 0) & (column == source + b), 1.0, 0.0).astype(BF16)
        for b in range(FOLD)
    ]
    blank = jnp.zeros((block, span), F32)
    for n in range(held.shape[0] // block):
        rows = slice(n * block, (n + 1) * block)
        total = None
        for left, right in pairs:
            term = dot(left[rows], right, 1, 1)
            total = term if total is None else total + term
        tail = total[:, main:].astype(BF16)
        moved = [dot(e, tail, 1, 0) for e in picks] + [blank]
        for c in range(2):
            lane = slice(c * DH, (c + 1) * DH)
            extra = jnp.concatenate(moved[2 * c : 2 * c + 2], axis=1)
            held[rows, lane] = (total[:, lane] + extra).astype(BF16)
        held[rows, 2 * DH :] = total[:, 2 * DH : main].astype(BF16)
        ship(held.at[rows], rows)


def weight_sum(ins, outs, scale):
    total = add_up(planes(ins[0])) * scale
    span = 2 * DH + DV - total.shape[1]
    outs[0][...] = total[:SHARE, :DH]
    outs[1][...] = total[:SHARE, DH : 2 * DH]
    outs[2][:, : DV - span] = total[:SHARE, 2 * DH :]
    for r in range(SHARE):
        a, b = SHARE + r // FOLD, r % FOLD
        outs[2][r : r + 1, DV - span :] = total[a : a + 1, b * span : (b + 1) * span]


def feature_sum(ins, outs):
    outs[0][...] = add_up(planes(ins[0])).astype(BF16)


def spread(ins, outs):
    own, low, high, taps = ins
    width = own.shape[1]
    body = own[...].astype(F32)
    padded = jnp.concatenate([low[...].astype(F32), body, high[...].astype(F32)], axis=1)
    summed = body
    for t in range(5):
        start = width - (t - 2) * DILATION_STEP
        summed = summed + taps[:, t : t + 1] * padded[:, start : start + width]
    outs[0][...] = summed


def local(tokens, conv_taps, w_query, w_key, w_value, grad_out):
    x = tokens[0]
    rows, columns = x.shape
    k_count = lax.axis_size(KGROUP)
    bx, core, sx, y = (lax.axis_size(a) for a in ("bx", "core", "sx", "y"))
    rest = bx * y
    share = columns // (bx * core * sx * y)
    heads = lax.axis_size("heads")
    slice_width = columns // heads
    width = 2 * DH + DV
    packed = width - DV % DH

    low, high = shift_pair(x[rows - REACH :], x[:REACH], SEQ)
    weights = jnp.concatenate([w_query, w_key, w_value], axis=1)
    (inner,) = call(blend, [((rows, columns), F32)], x, conv_taps, name="blend")
    blended, qdo, kv_all = call(
        lambda *a: project(*a, k_count),
        [((rows, columns), BF16), ((DH + DV, rows), BF16), ((k_count, DH + DV, rows), BF16)],
        inner, low, high, conv_taps, weights, grad_out[0].T,
        name="project", staged=((DH + DV, rows), k_count),
    )
    kv = exchange(kv_all, KGROUP)
    qdos = [qdo, swap(qdo, QGROUP)]

    groups = blended.reshape(rows, bx, core, sx, y, share)
    groups = jnp.pad(groups, ((0, 0),) * 5 + ((0, PAD - share),))
    groups = groups.transpose(2, 3, 1, 4, 5, 0).reshape(core, sx, rest * PAD, rows)
    mine = lax.axis_index("core")
    side = lax.axis_index("sx")
    kept = lax.dynamic_index_in_dim(groups, mine, 0, False)
    got = swap(lax.dynamic_index_in_dim(groups, 1 - mine, 0, False), "core")
    own = lax.dynamic_index_in_dim(kept, side, 0, False)
    near = lax.dynamic_index_in_dim(got, side, 0, False)
    crossing = jnp.stack(
        [
            lax.dynamic_index_in_dim(kept, 1 - side, 0, False),
            lax.dynamic_index_in_dim(got, 1 - side, 0, False),
        ]
    )
    kv, own, near, crossing = lax.optimization_barrier((kv, own, near, crossing))

    stats, exponents, products = call(
        statistics,
        [((8, sx * rows), F32)] + [((k_count * rows, sx * rows), F32)] * 2,
        kv, *qdos,
        name="statistics",
    )
    *odq, dkv = call(
        attend,
        [((DH + DV, rows), BF16)] * sx + [((k_count, DH + DV, rows), BF16)],
        kv, exponents, products, *qdos, stats, swap(stats, QGROUP),
        name="attend", staged=((k_count, DH + DV, rows), k_count),
    )
    dkv, far = lax.optimization_barrier((exchange(dkv, KGROUP), swap(crossing, "sx")))
    attended, grads, feature = call(
        features,
        [((DV, rows), BF16), ((width, rows), BF16), ((heads, slice_width, rows), BF16)],
        dkv, weights, odq[0], swap(odq[1], QGROUP),
        name="features", staged=((heads, slice_width, rows), heads),
    )
    far_grads = swap(grads, "sx")
    near_grads = swap(jnp.stack([grads, far_grads]), "core")
    feature = exchange(feature, "heads")
    (product,) = call(
        outer, [((rest * PAD, packed), BF16)],
        own, near, far, grads, far_grads, near_grads,
        name="outer", staged=((rest * PAD, packed), rest * PAD // 128),
    )
    product = exchange(product.reshape(rest, PAD, packed), REST)

    (own,) = call(feature_sum, [((slice_width, rows), BF16)], feature, name="feature_sum")
    before, after = shift_pair(own, own, SEQ)
    taps = lax.dynamic_slice_in_dim(
        conv_taps, lax.axis_index("heads") * slice_width, slice_width, 1
    ).T
    (grad_tokens,) = call(
        spread, [((slice_width, rows), F32)], own, before, after, taps, name="spread"
    )
    scale = 1.0 / math.sqrt(bx * core * sx * y * rows)
    grad_query, grad_key, grad_value = call(
        lambda i, o: weight_sum(i, o, scale),
        [((share, DH), F32), ((share, DH), F32), ((share, DV), F32)],
        product,
        name="weight_sum",
    )
    return attended.T[None], grad_tokens.T[None], grad_query, grad_key, grad_value


def split(mesh):
    batch, heads, seq = mesh.devices.shape
    shape = (batch // 2, 2, heads, 2, seq // 2)
    return Mesh(mesh.devices.reshape(shape), ("bx", "core", "heads", "sx", "y"))


def solution(mesh):
    batch = ("bx", "core")
    whole = split(mesh)
    return jax.shard_map(
        local,
        mesh=whole,
        in_specs=(
            P(batch, SEQ, None),
            P(),
            P(None, "heads"),
            P(None, "heads"),
            P(None, "heads"),
            P(batch, SEQ, "heads"),
        ),
        out_specs=(
            P(batch, SEQ, "heads"),
            P(batch, SEQ, "heads"),
            P(batch + SEQ, "heads"),
            P(batch + SEQ, "heads"),
            P(batch + SEQ, "heads"),
        ),
        check_vma=False,
    )
```

```python
import math

import jax
import jax.numpy as jnp
from jax import lax
from jax.experimental import pallas as pl
from jax.experimental.pallas import tpu as pltpu
from jax.sharding import Mesh
from jax.sharding import PartitionSpec as P

DH = 128
DV = 192
DILATION_STEP = 4
REACH = 2 * DILATION_STEP
PAD = 16
SHARE = 12
FOLD = 3
VMEM = 16 << 20

F32 = jnp.float32
BF16 = jnp.bfloat16
SEQ = ("sx", "y")
QGROUP = "sx"
KGROUP = "y"
REST = ("bx", "y")


def dot(a, b, ca, cb):
    return lax.dot_general(a, b, (((ca,), (cb,)), ((), ())), preferred_element_type=F32)


def call(body, outs, *args, name, staged=None):
    count = len(args)

    def kernel(*refs):
        ins, results = refs[:count], refs[count : count + len(outs)]
        if staged is None:
            body(ins, results)
            return
        held, sems = refs[-2], refs[-1]
        target = results[-1]
        copies = []

        def ship(source, place):
            if copies:
                copies[-1].start()
            copies.append(
                pltpu.make_async_copy(source, target.at[place], sems.at[len(copies)])
            )

        body(ins, results[:-1], held, ship)
        copies[-1].start()
        for copy in copies:
            copy.wait()

    near = pl.BlockSpec(memory_space=pltpu.VMEM)
    specs = [near] * len(outs)
    scratch = []
    if staged is not None:
        shape, pieces = staged
        specs[-1] = pl.BlockSpec(memory_space=pl.ANY)
        scratch = [pltpu.VMEM(shape, outs[-1][1]), pltpu.SemaphoreType.DMA((pieces,))]
    return pl.pallas_call(
        kernel,
        out_shape=[jax.ShapeDtypeStruct(s, t) for s, t in outs],
        in_specs=[near] * count,
        out_specs=specs,
        scratch_shapes=scratch,
        name=name,
        compiler_params=pltpu.CompilerParams(vmem_limit_bytes=VMEM),
    )(*args)


def exchange(x, axis):
    return lax.all_to_all(x, axis, split_axis=0, concat_axis=0, tiled=True)


def swap(x, axis):
    return lax.ppermute(x, axis, [(0, 1), (1, 0)])


def gather_pair(x):
    far = swap(x, "sx")
    return x, far, swap(jnp.stack([x, far]), "core")


def shift_pair(low_source, high_source, axes):
    count = lax.axis_size(axes)
    forward = [(i, i + 1) for i in range(count - 1)]
    backward = [(j, i) for i, j in forward]
    return lax.ppermute(low_source, axes, forward), lax.ppermute(high_source, axes, backward)


def blend(ins, outs):
    tokens, taps = ins
    rows, columns = tokens.shape
    body = tokens[...].astype(F32)
    edge = jnp.zeros((REACH, columns), F32)
    padded = jnp.concatenate([edge, body, edge], axis=0)
    summed = body
    for t in range(5):
        summed = summed + taps[t : t + 1, :] * padded[t * DILATION_STEP : t * DILATION_STEP + rows]
    outs[0][...] = summed


def project(ins, outs):
    inner, low, high, taps, weights, do = ins
    blended_out, qdo, kv_out = outs
    rows, columns = inner.shape
    low = low[...].astype(F32)
    high = high[...].astype(F32)
    none = jnp.zeros((DILATION_STEP, columns), F32)
    first = taps[0:1] * low + jnp.concatenate([taps[1:2] * low[DILATION_STEP:], none], axis=0)
    last = taps[4:5] * high + jnp.concatenate([none, taps[3:4] * high[:DILATION_STEP]], axis=0)
    summed = jnp.concatenate(
        [inner[:REACH] + first, inner[REACH : rows - REACH], inner[rows - REACH :] + last], axis=0
    )
    blended = summed.astype(BF16)
    qkv = dot(blended, weights[...], 1, 0).T.astype(BF16)
    blended_out[...] = blended
    qdo[:DH] = qkv[:DH]
    qdo[DH:] = do[...]
    for n in range(kv_out.shape[0]):
        kv_out[n] = qkv[DH:]


def lanes(ref, first, last):
    return jnp.concatenate([ref[n, first:last] for n in range(ref.shape[0])], axis=1)


SCALE = 1.0 / math.sqrt(DH)


def statistics(ins, outs):
    kv, qdos = ins[0], ins[1:]
    stats, exponents, products = outs
    k_rows = lanes(kv, 0, DH).T
    v_rows = lanes(kv, DH, DH + DV).T
    width = qdos[0].shape[1]
    for m, qdo in enumerate(qdos):
        s = dot(k_rows, qdo[:DH], 1, 0) * SCALE
        top = jnp.max(s, axis=0, keepdims=True)
        e = jnp.exp(s - top)
        total = jnp.sum(e, axis=0, keepdims=True)
        dp = dot(v_rows, qdo[DH:], 1, 0)
        weighted = jnp.sum(e * dp, axis=0, keepdims=True)
        part = jnp.concatenate([top, total, weighted, jnp.zeros((5, width), F32)], axis=0)
        lane = slice(m * width, (m + 1) * width)
        stats[:, lane] = part
        exponents[:, lane] = e
        products[:, lane] = dp


def attend(ins, outs, dkv, ship):
    kv, exponents, products = ins[:3]
    blocks = len(outs)
    qdos, stats = ins[3 : 3 + blocks], ins[3 + blocks :]
    odq = outs
    kt = lanes(kv, 0, DH)
    vt = lanes(kv, DH, DH + DV)
    width = qdos[0].shape[1]
    dk = dv = None
    for m, qdo in enumerate(qdos):
        part = [stats[c][:, (m ^ c) * width : ((m ^ c) + 1) * width] for c in range(blocks)]
        top = part[0][0:1]
        for x in part[1:]:
            top = jnp.maximum(top, x[0:1])
        total = jnp.zeros_like(top)
        weighted = jnp.zeros_like(top)
        for x in part:
            factor = jnp.exp(x[0:1] - top)
            total = total + factor * x[1:2]
            weighted = weighted + factor * x[2:3]
        row_dots = weighted / total
        lane = slice(m * width, (m + 1) * width)
        a = exponents[:, lane] * (jnp.exp(part[0][0:1] - top) / total)
        ab = a.astype(BF16)
        ds = (a * (products[:, lane] - row_dots) * SCALE).astype(BF16)
        odq[m][:DV] = dot(vt, ab, 1, 0).astype(BF16)
        odq[m][DV:] = dot(kt, ds, 1, 0).astype(BF16)
        dk_m = dot(qdo[:DH], ds, 1, 1)
        dv_m = dot(qdo[DH:], ab, 1, 1)
        dk = dk_m if dk is None else dk + dk_m
        dv = dv_m if dv is None else dv + dv_m
    for n in range(dkv.shape[0]):
        dkv[n, :DH] = dk[:, n * width : (n + 1) * width].astype(BF16)
        dkv[n, DH:] = dv[:, n * width : (n + 1) * width].astype(BF16)
        ship(dkv.at[n], n)


def add_up(pieces):
    total = pieces[0][...].astype(F32)
    for x in pieces[1:]:
        total = total + x[...].astype(F32)
    return total


def planes(ref):
    return [ref.at[n] for n in range(ref.shape[0])]


def query_side(ins, outs):
    total = add_up(ins)
    outs[0][...] = total[:DV].astype(BF16)
    outs[1][...] = total[DV:].astype(BF16)


def features(ins, outs):
    dkv, dq, weights = ins
    grads, feature = outs
    total = add_up(planes(dkv)).astype(BF16)
    grads[...] = total
    every = jnp.concatenate([dq[...], total], axis=0)
    feature[...] = dot(weights[...], every, 1, 0).astype(BF16)


def product_of(ins, rows):
    own, near, far, grads, far_grads, near_grads = ins
    pairs = [
        (own, grads[...]),
        (near, near_grads[0]),
        (far.at[0], far_grads[...]),
        (far.at[1], near_grads[1]),
    ]
    total = None
    for left, right in pairs:
        term = dot(left[rows], right, 1, 1)
        total = term if total is None else total + term
    return total


def query_product(ins, outs):
    outs[0][...] = product_of(ins, slice(None)).astype(BF16)


def outer(ins, outs):
    (packed,) = outs
    first = ins[-1]
    block = 128
    row = lax.broadcasted_iota(jnp.int32, (block, block), 0)
    column = lax.broadcasted_iota(jnp.int32, (block, block), 1)
    spare = (row & (PAD - 1)) - SHARE
    source = row - (row & (PAD - 1)) + FOLD * spare
    picks = [
        jnp.where((spare >= 0) & (column == source + b), 1.0, 0.0).astype(BF16)
        for b in range(FOLD)
    ]
    total = product_of(ins[:-1], slice(None))
    main = 2 * DH
    tail = total[:, main:].astype(BF16)
    blank = jnp.zeros((block, total.shape[1] - main), F32)
    for n in range(packed.shape[0] // block):
        rows = slice(n * block, (n + 1) * block)
        moved = [dot(e, tail[rows], 1, 0) for e in picks] + [blank]
        extra = [jnp.concatenate(moved[c : c + 2], axis=1) for c in (0, 2)]
        packed[rows, :DH] = (first[rows].astype(F32) + extra[0]).astype(BF16)
        packed[rows, DH : 2 * DH] = (total[rows, :DH] + extra[1]).astype(BF16)
        packed[rows, 2 * DH :] = total[rows, DH:main].astype(BF16)


def weight_sum(ins, outs, scale):
    total = add_up(planes(ins[0])) * scale
    span = 2 * DH + DV - total.shape[1]
    outs[0][...] = total[:SHARE, :DH]
    outs[1][...] = total[:SHARE, DH : 2 * DH]
    outs[2][:, : DV - span] = total[:SHARE, 2 * DH :]
    for r in range(SHARE):
        a, b = SHARE + r // FOLD, r % FOLD
        outs[2][r : r + 1, DV - span :] = total[a : a + 1, b * span : (b + 1) * span]


def feature_sum(ins, outs):
    outs[0][...] = add_up(planes(ins[0])).astype(BF16)


def spread(ins, outs):
    own, low, high, taps = ins
    width = own.shape[1]
    body = own[...].astype(F32)
    padded = jnp.concatenate([low[...].astype(F32), body, high[...].astype(F32)], axis=1)
    summed = body
    for t in range(5):
        start = width - (t - 2) * DILATION_STEP
        summed = summed + taps[:, t : t + 1] * padded[:, start : start + width]
    outs[0][...] = summed


def local(tokens, conv_taps, w_query, w_key, w_value, grad_out):
    x = tokens[0]
    rows, columns = x.shape
    k_count = lax.axis_size(KGROUP)
    bx, core, sx, y = (lax.axis_size(a) for a in ("bx", "core", "sx", "y"))
    rest = bx * y
    share = columns // (bx * core * sx * y)
    heads = lax.axis_size("heads")
    slice_width = columns // heads
    width = 2 * DH + DV
    packed = width - DV % DH

    low, high = shift_pair(x[rows - REACH :], x[:REACH], SEQ)
    weights = jnp.concatenate([w_query, w_key, w_value], axis=1)
    (inner,) = call(blend, [((rows, columns), F32)], x, conv_taps, name="blend")
    blended, qdo, kv_all = call(
        project,
        [((rows, columns), BF16), ((DH + DV, rows), BF16), ((k_count, DH + DV, rows), BF16)],
        inner, low, high, conv_taps, weights, grad_out[0].T,
        name="project",
    )
    kv = exchange(kv_all, KGROUP)
    qdos = [qdo, swap(qdo, QGROUP)]

    groups = blended.reshape(rows, bx, core, sx, y, share)
    groups = jnp.pad(groups, ((0, 0),) * 5 + ((0, PAD - share),))
    groups = groups.transpose(2, 3, 1, 4, 5, 0).reshape(core, sx, rest * PAD, rows)
    mine = lax.axis_index("core")
    side = lax.axis_index("sx")
    kept = lax.dynamic_index_in_dim(groups, mine, 0, False)
    got = swap(lax.dynamic_index_in_dim(groups, 1 - mine, 0, False), "core")
    own = lax.dynamic_index_in_dim(kept, side, 0, False)
    near = lax.dynamic_index_in_dim(got, side, 0, False)
    crossing = jnp.stack(
        [
            lax.dynamic_index_in_dim(kept, 1 - side, 0, False),
            lax.dynamic_index_in_dim(got, 1 - side, 0, False),
        ]
    )
    kv, own, near, crossing = lax.optimization_barrier((kv, own, near, crossing))

    stats, exponents, products = call(
        statistics,
        [((8, sx * rows), F32)] + [((k_count * rows, sx * rows), F32)] * 2,
        kv, *qdos,
        name="statistics",
    )
    *odq, dkv = call(
        attend,
        [((DH + DV, rows), BF16)] * sx + [((k_count, DH + DV, rows), BF16)],
        kv, exponents, products, *qdos, stats, swap(stats, QGROUP),
        name="attend", staged=((k_count, DH + DV, rows), k_count),
    )
    far = swap(crossing, "sx")
    attended, dq = call(
        query_side,
        [((DV, rows), BF16), ((DH, rows), BF16)],
        odq[0], swap(odq[1], QGROUP),
        name="query_side",
    )
    (first,) = call(
        query_product, [((rest * PAD, DH), BF16)],
        own, near, far, *gather_pair(dq),
        name="query_product",
    )
    dkv, far, first = lax.optimization_barrier((exchange(dkv, KGROUP), far, first))
    grads, feature = call(
        features,
        [((DH + DV, rows), BF16), ((columns, rows), BF16)],
        dkv, dq, weights,
        name="features",
    )
    right = gather_pair(grads)
    feature = exchange(feature.reshape(heads, slice_width, rows), "heads")
    (product,) = call(
        outer, [((rest * PAD, packed), BF16)],
        own, near, far, *right, first,
        name="outer",
    )
    product = exchange(product.reshape(rest, PAD, packed), REST)

    (own,) = call(feature_sum, [((slice_width, rows), BF16)], feature, name="feature_sum")
    before, after = shift_pair(own, own, SEQ)
    taps = lax.dynamic_slice_in_dim(
        conv_taps, lax.axis_index("heads") * slice_width, slice_width, 1
    ).T
    (grad_tokens,) = call(
        spread, [((slice_width, rows), F32)], own, before, after, taps, name="spread"
    )
    scale = 1.0 / math.sqrt(bx * core * sx * y * rows)
    grad_query, grad_key, grad_value = call(
        lambda i, o: weight_sum(i, o, scale),
        [((share, DH), F32), ((share, DH), F32), ((share, DV), F32)],
        product,
        name="weight_sum",
    )
    return attended.T[None], grad_tokens.T[None], grad_query, grad_key, grad_value


def split(mesh):
    batch, heads, seq = mesh.devices.shape
    shape = (batch // 2, 2, heads, 2, seq // 2)
    return Mesh(mesh.devices.reshape(shape), ("bx", "core", "heads", "sx", "y"))


def solution(mesh):
    batch = ("bx", "core")
    whole = split(mesh)
    return jax.shard_map(
        local,
        mesh=whole,
        in_specs=(
            P(batch, SEQ, None),
            P(),
            P(None, "heads"),
            P(None, "heads"),
            P(None, "heads"),
            P(batch, SEQ, "heads"),
        ),
        out_specs=(
            P(batch, SEQ, "heads"),
            P(batch, SEQ, "heads"),
            P(batch + SEQ, "heads"),
            P(batch + SEQ, "heads"),
            P(batch + SEQ, "heads"),
        ),
        check_vma=False,
    )
```

```python
import math

import jax
import jax.numpy as jnp
from jax import lax
from jax.experimental import pallas as pl
from jax.experimental.pallas import tpu as pltpu
from jax.sharding import Mesh
from jax.sharding import PartitionSpec as P

DH = 128
DV = 192
DILATION_STEP = 4
REACH = 2 * DILATION_STEP
PAD = 16
SHARE = 12
FOLD = 3
VMEM = 16 << 20

F32 = jnp.float32
BF16 = jnp.bfloat16
SEQ = ("sx", "y")
QGROUP = "y"
KGROUP = "sx"
REST = ("bx", "y")


def dot(a, b, ca, cb):
    return lax.dot_general(a, b, (((ca,), (cb,)), ((), ())), preferred_element_type=F32)


def call(body, outs, *args, name, scalars=0):
    def kernel(*refs):
        body(refs[: len(args)], refs[len(args) :])

    return pl.pallas_call(
        kernel,
        out_shape=[jax.ShapeDtypeStruct(s, t) for s, t in outs],
        in_specs=[pl.BlockSpec(memory_space=pltpu.SMEM)] * scalars
        + [pl.BlockSpec(memory_space=pltpu.VMEM)] * (len(args) - scalars),
        name=name,
        compiler_params=pltpu.CompilerParams(vmem_limit_bytes=VMEM),
    )(*args)


def exchange(x, axis):
    return lax.all_to_all(x, axis, split_axis=0, concat_axis=0, tiled=True)


def swap(x, axis, k=1):
    return lax.ppermute(x, axis, [(i, i ^ k) for i in range(lax.axis_size(axis))])


def shift_pair(low_source, high_source, axes):
    count = lax.axis_size(axes)
    forward = [(i, i + 1) for i in range(count - 1)]
    backward = [(j, i) for i, j in forward]
    return lax.ppermute(low_source, axes, forward), lax.ppermute(high_source, axes, backward)


def blend(ins, outs):
    tokens, taps = ins
    rows, columns = tokens.shape
    body = tokens[...].astype(F32)
    edge = jnp.zeros((REACH, columns), F32)
    padded = jnp.concatenate([edge, body, edge], axis=0)
    summed = body
    for t in range(5):
        summed = summed + taps[t : t + 1, :] * padded[t * DILATION_STEP : t * DILATION_STEP + rows]
    outs[0][...] = summed


def project(ins, outs):
    inner, low, high, taps, weights = ins
    blended_out, q_out, kv = outs
    rows, columns = inner.shape
    low = low[...].astype(F32)
    high = high[...].astype(F32)
    none = jnp.zeros((DILATION_STEP, columns), F32)
    first = taps[0:1] * low + jnp.concatenate([taps[1:2] * low[DILATION_STEP:], none], axis=0)
    last = taps[4:5] * high + jnp.concatenate([none, taps[3:4] * high[:DILATION_STEP]], axis=0)
    summed = jnp.concatenate(
        [inner[:REACH] + first, inner[REACH : rows - REACH], inner[rows - REACH :] + last], axis=0
    )
    blended = summed.astype(BF16)
    blended_out[...] = blended
    qkv = dot(blended, weights[...], 1, 0).T.astype(BF16)
    for n in range(q_out.shape[0]):
        q_out[n] = qkv[:DH]
    kv[...] = qkv[DH:]


SCALE = 1.0 / math.sqrt(DH)


def statistics(ins, outs):
    q, do, *kvs = ins
    (stats,) = outs
    k_rows = jnp.concatenate([kv[:DH].T for kv in kvs], axis=0)
    v_rows = jnp.concatenate([kv[DH:].T for kv in kvs], axis=0)
    blocks, _, width = q.shape
    tops, totals, sums = [], [], []
    for m in range(blocks):
        s = dot(k_rows, q[m], 1, 0) * SCALE
        top = jnp.max(s, axis=0, keepdims=True)
        e = jnp.exp(s - top)
        dp = dot(v_rows, do[m], 1, 0)
        tops.append(top)
        totals.append(jnp.sum(e, axis=0, keepdims=True))
        sums.append(jnp.sum(e * dp, axis=0, keepdims=True))
    part = jnp.concatenate(tops + totals + sums, axis=0)
    for c in range(stats.shape[0]):
        stats[c] = part


def attend(ins, outs):
    place, q, do, stats, *kvs = ins
    kept, sent, dq, dkv, crossing, tops, scales, dots = outs
    blocks, _, width = q.shape
    top = stats[0, :blocks]
    for c in range(1, blocks):
        top = jnp.maximum(top, stats[c, :blocks])
    total = jnp.zeros_like(top)
    weighted = jnp.zeros_like(top)
    for c in range(blocks):
        factor = jnp.exp(stats[c, :blocks] - top)
        total = total + factor * stats[c, blocks : 2 * blocks]
        weighted = weighted + factor * stats[c, 2 * blocks :]
    tops[...] = top
    scales[...] = 1.0 / total
    dots[...] = weighted / total
    kt = jnp.concatenate([kv[:DH] for kv in kvs], axis=1)
    vt = jnp.concatenate([kv[DH:] for kv in kvs], axis=1)
    k_rows = kt.T
    v_rows = vt.T
    own = place[0]
    dk = dv = None
    for j in range(blocks):
        m = own ^ j
        s = dot(k_rows, q[m], 1, 0) * SCALE
        a = jnp.exp(s - tops[pl.ds(m, 1), :]) * scales[pl.ds(m, 1), :]
        ab = a.astype(BF16)
        dp = dot(v_rows, do[m], 1, 0)
        ds = (a * (dp - dots[pl.ds(m, 1), :]) * SCALE).astype(BF16)
        attended = dot(vt, ab, 1, 0)
        if j % 2:
            sent[j // 2] = attended.astype(BF16)
        else:
            kept[j // 2] = attended
        dq[m] = dot(kt, ds, 1, 0).astype(BF16)
        dk_m = dot(q[m], ds, 1, 1)
        dv_m = dot(do[m], ab, 1, 1)
        dk = dk_m if dk is None else dk + dk_m
        dv = dv_m if dv is None else dv + dv_m
    every = jnp.concatenate([dk, dv], axis=0)
    dkv[...] = every[:, :width]
    crossing[...] = every[:, width:].astype(BF16)


def fold(ins, outs):
    kept, came = ins
    keep, send = outs
    for n in range(kept.shape[0]):
        total = kept[n] + came[n].astype(F32)
        if n % 2:
            send[n // 2] = total.astype(BF16)
        else:
            keep[n // 2] = total


def finish(ins, outs):
    kept, came = ins
    outs[0][...] = (kept[0] + came[0].astype(F32)).astype(BF16)


def add_up(pieces):
    total = pieces[0][...].astype(F32)
    for x in pieces[1:]:
        total = total + x[...].astype(F32)
    return total


def planes(ref):
    return [ref.at[n] for n in range(ref.shape[0])]


def features(ins, outs):
    dq, dkv, came, weights = ins
    grads, feature = outs
    first = add_up(planes(dq)).astype(BF16)
    second = add_up([dkv, came]).astype(BF16)
    every = jnp.concatenate([first, second], axis=0)
    grads[...] = every
    feature[...] = dot(weights[...], every, 1, 0).astype(BF16)


def outer(ins, outs):
    own, near, far, grads, far_grads, near_grads = ins
    pairs = [
        (own[...], grads[...]),
        (near[...], near_grads[0]),
        (far[0], far_grads[...]),
        (far[1], near_grads[1]),
    ]
    total = None
    for left, right in pairs:
        term = dot(left, right, 1, 1)
        total = term if total is None else total + term
    main = outs[0].shape[1]
    span = total.shape[1] - main
    block = 128
    row = lax.broadcasted_iota(jnp.int32, (block, block), 0)
    column = lax.broadcasted_iota(jnp.int32, (block, block), 1)
    spare = (row & (PAD - 1)) - SHARE
    source = row - (row & (PAD - 1)) + FOLD * spare
    picks = [
        jnp.where((spare >= 0) & (column == source + b), 1.0, 0.0).astype(BF16)
        for b in range(FOLD)
    ]
    tail = total[:, main:].astype(BF16)
    blank = jnp.zeros((block, span), F32)
    for n in range(total.shape[0] // block):
        rows = slice(n * block, (n + 1) * block)
        moved = [dot(e, tail[rows], 1, 0) for e in picks] + [blank]
        for c in range(2):
            lane = slice(c * DH, (c + 1) * DH)
            extra = jnp.concatenate(moved[2 * c : 2 * c + 2], axis=1)
            outs[0][rows, lane] = (total[rows, lane] + extra).astype(BF16)
        outs[0][rows, 2 * DH :] = total[rows, 2 * DH : main].astype(BF16)


def weight_sum(ins, outs, scale):
    total = add_up(planes(ins[0])) * scale
    span = 2 * DH + DV - total.shape[1]
    outs[0][...] = total[:SHARE, :DH]
    outs[1][...] = total[:SHARE, DH : 2 * DH]
    outs[2][:, : DV - span] = total[:SHARE, 2 * DH :]
    for r in range(SHARE):
        a, b = SHARE + r // FOLD, r % FOLD
        outs[2][r : r + 1, DV - span :] = total[a : a + 1, b * span : (b + 1) * span]


def feature_sum(ins, outs):
    outs[0][...] = add_up(planes(ins[0])).astype(BF16)


def spread(ins, outs):
    own, low, high, taps = ins
    width = own.shape[1]
    body = own[...].astype(F32)
    padded = jnp.concatenate([low[...].astype(F32), body, high[...].astype(F32)], axis=1)
    summed = body
    for t in range(5):
        start = width - (t - 2) * DILATION_STEP
        summed = summed + taps[:, t : t + 1] * padded[:, start : start + width]
    outs[0][...] = summed


def local(tokens, conv_taps, w_query, w_key, w_value, grad_out):
    x = tokens[0]
    rows, columns = x.shape
    count = lax.axis_size(QGROUP)
    bx, core, sx, y = (lax.axis_size(a) for a in ("bx", "core", "sx", "y"))
    rest = bx * y
    share = columns // (bx * core * sx * y)
    heads = lax.axis_size("heads")
    slice_width = columns // heads
    width = 2 * DH + DV
    packed = width - DV % DH

    do = exchange(jnp.broadcast_to(grad_out[0].T[None], (count, DV, rows)), QGROUP)
    low, high = shift_pair(x[rows - REACH :], x[:REACH], SEQ)
    weights = jnp.concatenate([w_query, w_key, w_value], axis=1)
    (inner,) = call(blend, [((rows, columns), F32)], x, conv_taps, name="blend")
    blended, q_all, kv = call(
        project,
        [((rows, columns), BF16), ((count, DH, rows), BF16), ((DH + DV, rows), BF16)],
        inner, low, high, conv_taps, weights,
        name="project",
    )
    q_all, do = lax.optimization_barrier((q_all, do))
    q = exchange(q_all, QGROUP)
    kvs = [kv, swap(kv, KGROUP)]

    groups = blended.reshape(rows, bx, core, sx, y, share)
    groups = jnp.pad(groups, ((0, 0),) * 5 + ((0, PAD - share),))
    groups = groups.transpose(2, 3, 1, 4, 5, 0).reshape(core, sx, rest * PAD, rows)
    mine = lax.axis_index("core")
    side = lax.axis_index("sx")
    kept = lax.dynamic_index_in_dim(groups, mine, 0, False)
    got = swap(lax.dynamic_index_in_dim(groups, 1 - mine, 0, False), "core")
    own = lax.dynamic_index_in_dim(kept, side, 0, False)
    near = lax.dynamic_index_in_dim(got, side, 0, False)
    crossing = jnp.stack(
        [
            lax.dynamic_index_in_dim(kept, 1 - side, 0, False),
            lax.dynamic_index_in_dim(got, 1 - side, 0, False),
        ]
    )
    q, own, near, crossing = lax.optimization_barrier((q, own, near, crossing))

    (stats,) = call(
        statistics, [((count, 3 * count, rows), F32)], q, do, *kvs, name="statistics"
    )
    stats = exchange(stats, QGROUP)
    place = lax.axis_index(QGROUP).reshape(1).astype(jnp.int32)
    kept, sent, dq, dkv, other, _, _, _ = call(
        attend,
        [
            ((count // 2, DV, rows), F32),
            ((count // 2, DV, rows), BF16),
            ((count, DH, rows), BF16),
            ((DH + DV, rows), F32),
            ((DH + DV, rows), BF16),
        ]
        + [((count, rows), F32)] * 3,
        place, q, do, stats, *kvs,
        name="attend", scalars=1,
    )
    dq = exchange(dq, QGROUP)
    far = swap(crossing, "sx")
    came = swap(other, KGROUP)
    step, size = 1, count // 2
    while size > 1:
        size //= 2
        kept, sent = call(
            fold,
            [((size, DV, rows), F32), ((size, DV, rows), BF16)],
            kept, swap(sent, QGROUP, step),
            name="fold",
        )
        if step == 1:
            dq, kept, sent = lax.optimization_barrier((dq, kept, sent))
        step *= 2
    (attended,) = call(
        finish, [((DV, rows), BF16)], kept, swap(sent, QGROUP, step), name="finish"
    )
    dq, far = lax.optimization_barrier((dq, far))
    grads, feature = call(
        features,
        [((width, rows), BF16), ((columns, rows), BF16)],
        dq, dkv, came, weights,
        name="features",
    )
    far_grads = swap(grads, "sx")
    near_grads = swap(jnp.stack([grads, far_grads]), "core")
    feature = exchange(feature.reshape(heads, slice_width, rows), "heads")
    (product,) = call(
        outer, [((rest * PAD, packed), BF16)],
        own, near, far, grads, far_grads, near_grads,
        name="outer",
    )
    product = exchange(product.reshape(rest, PAD, packed), REST)

    (own,) = call(feature_sum, [((slice_width, rows), BF16)], feature, name="feature_sum")
    before, after = shift_pair(own, own, SEQ)
    taps = lax.dynamic_slice_in_dim(
        conv_taps, lax.axis_index("heads") * slice_width, slice_width, 1
    ).T
    (grad_tokens,) = call(
        spread, [((slice_width, rows), F32)], own, before, after, taps, name="spread"
    )
    scale = 1.0 / math.sqrt(bx * core * sx * y * rows)
    grad_query, grad_key, grad_value = call(
        lambda i, o: weight_sum(i, o, scale),
        [((share, DH), F32), ((share, DH), F32), ((share, DV), F32)],
        product,
        name="weight_sum",
    )
    return attended.T[None], grad_tokens.T[None], grad_query, grad_key, grad_value


def split(mesh):
    batch, heads, seq = mesh.devices.shape
    shape = (batch // 2, 2, heads, 2, seq // 2)
    return Mesh(mesh.devices.reshape(shape), ("bx", "core", "heads", "sx", "y"))


def solution(mesh):
    batch = ("bx", "core")
    whole = split(mesh)
    return jax.shard_map(
        local,
        mesh=whole,
        in_specs=(
            P(batch, SEQ, None),
            P(),
            P(None, "heads"),
            P(None, "heads"),
            P(None, "heads"),
            P(batch, SEQ, "heads"),
        ),
        out_specs=(
            P(batch, SEQ, "heads"),
            P(batch, SEQ, "heads"),
            P(batch + SEQ, "heads"),
            P(batch + SEQ, "heads"),
            P(batch + SEQ, "heads"),
        ),
        check_vma=False,
    )
```

```python
import math

import jax
import jax.numpy as jnp
from jax import lax
from jax.experimental import pallas as pl
from jax.experimental.pallas import tpu as pltpu
from jax.sharding import Mesh
from jax.sharding import PartitionSpec as P

DH = 128
DV = 192
DILATION_STEP = 4
REACH = 2 * DILATION_STEP
PAD = 16
SHARE = 12
FOLD = 3
VMEM = 16 << 20

F32 = jnp.float32
BF16 = jnp.bfloat16
SEQ = ("sx", "yh", "yl")
QGROUP = ("sx", "yl")
KGROUP = "yh"
REST = ("bx", "yh", "yl")
ORDER = (0, 2, 1, 3)


def dot(a, b, ca, cb):
    return lax.dot_general(a, b, (((ca,), (cb,)), ((), ())), preferred_element_type=F32)


def call(body, outs, *args, scalars=0):
    def kernel(*refs):
        body(refs[: len(args)], refs[len(args) :])

    return pl.pallas_call(
        kernel,
        out_shape=[jax.ShapeDtypeStruct(s, t) for s, t in outs],
        in_specs=[pl.BlockSpec(memory_space=pltpu.SMEM)] * scalars
        + [pl.BlockSpec(memory_space=pltpu.VMEM)] * (len(args) - scalars),
        compiler_params=pltpu.CompilerParams(vmem_limit_bytes=VMEM),
    )(*args)


def exchange(x, axis):
    return lax.all_to_all(x, axis, split_axis=0, concat_axis=0, tiled=True)


def swap(x, axis):
    return lax.ppermute(x, axis, [(0, 1), (1, 0)])


def shift_pair(low_source, high_source, axes):
    count = lax.axis_size(axes)
    forward = [(i, i + 1) for i in range(count - 1)]
    backward = [(j, i) for i, j in forward]
    return lax.ppermute(low_source, axes, forward), lax.ppermute(high_source, axes, backward)


def blend(ins, outs):
    tokens, taps = ins
    rows, columns = tokens.shape
    body = tokens[...].astype(F32)
    edge = jnp.zeros((REACH, columns), F32)
    padded = jnp.concatenate([edge, body, edge], axis=0)
    summed = body
    for t in range(5):
        summed = summed + taps[t : t + 1, :] * padded[t * DILATION_STEP : t * DILATION_STEP + rows]
    outs[0][...] = summed


def project(ins, outs):
    inner, low, high, taps, weights, do = ins
    blended_out, qdo, kv_out = outs
    rows, columns = inner.shape
    low = low[...].astype(F32)
    high = high[...].astype(F32)
    none = jnp.zeros((DILATION_STEP, columns), F32)
    first = taps[0:1] * low + jnp.concatenate([taps[1:2] * low[DILATION_STEP:], none], axis=0)
    last = taps[4:5] * high + jnp.concatenate([none, taps[3:4] * high[:DILATION_STEP]], axis=0)
    summed = jnp.concatenate(
        [inner[:REACH] + first, inner[REACH : rows - REACH], inner[rows - REACH :] + last], axis=0
    )
    blended = summed.astype(BF16)
    blended_out[...] = blended
    qkv = dot(blended, weights[...], 1, 0).T.astype(BF16)
    qdo[:DH] = qkv[:DH]
    qdo[DH:] = do[...]
    for n in range(kv_out.shape[0]):
        kv_out[n] = qkv[DH:]


def lanes(ref, first, last):
    return jnp.concatenate([ref[n, first:last] for n in range(ref.shape[0])], axis=1)


SCALE = 1.0 / math.sqrt(DH)


def statistics(ins, outs):
    place, kv, own, near, far = ins
    qdos = [own, near, far.at[0], far.at[1]]
    (stats,) = outs
    k_rows = lanes(kv, 0, DH).T
    v_rows = lanes(kv, DH, DH + DV).T
    width = own.shape[1]
    for j, qdo in enumerate(qdos):
        s = dot(k_rows, qdo[:DH], 1, 0) * SCALE
        top = jnp.max(s, axis=0, keepdims=True)
        e = jnp.exp(s - top)
        total = jnp.sum(e, axis=0, keepdims=True)
        dp = dot(v_rows, qdo[DH:], 1, 0)
        weighted = jnp.sum(e * dp, axis=0, keepdims=True)
        part = jnp.concatenate([top, total, weighted, jnp.zeros((5, width), F32)], axis=0)
        m = place[0] ^ ORDER[j]
        for c in range(stats.shape[0]):
            stats[c, m] = part


def attend(ins, outs):
    place, kv, own, near, far, stats = ins
    qdos = [own, near, far.at[0], far.at[1]]
    kept, nearby, sent, dkv = outs
    kt = lanes(kv, 0, DH)
    vt = lanes(kv, DH, DH + DV)
    k_rows = kt.T
    v_rows = vt.T
    width = own.shape[1]
    dk = dv = None
    for j, qdo in enumerate(qdos):
        m = place[0] ^ ORDER[j]
        part = [stats[c, m] for c in range(stats.shape[0])]
        top = part[0][0:1]
        for x in part[1:]:
            top = jnp.maximum(top, x[0:1])
        total = jnp.zeros_like(top)
        weighted = jnp.zeros_like(top)
        for x in part:
            factor = jnp.exp(x[0:1] - top)
            total = total + factor * x[1:2]
            weighted = weighted + factor * x[2:3]
        row_dots = weighted / total
        s = dot(k_rows, qdo[:DH], 1, 0) * SCALE
        a = jnp.exp(s - top) / total
        ab = a.astype(BF16)
        dp = dot(v_rows, qdo[DH:], 1, 0)
        ds = (a * (dp - row_dots) * SCALE).astype(BF16)
        piece = jnp.concatenate([dot(vt, ab, 1, 0), dot(kt, ds, 1, 0)], axis=0)
        if j < 2:
            (kept, nearby)[j][...] = piece
        else:
            sent[j - 2] = piece.astype(BF16)
        dk_m = dot(qdo[:DH], ds, 1, 1)
        dv_m = dot(qdo[DH:], ab, 1, 1)
        dk = dk_m if dk is None else dk + dk_m
        dv = dv_m if dv is None else dv + dv_m
    for n in range(dkv.shape[0]):
        dkv[n, :DH] = dk[:, n * width : (n + 1) * width].astype(BF16)
        dkv[n, DH:] = dv[:, n * width : (n + 1) * width].astype(BF16)


def fold(ins, outs):
    kept, nearby, came = ins
    outs[0][...] = kept[...] + came[0].astype(F32)
    outs[1][...] = (nearby[...] + came[1].astype(F32)).astype(BF16)


def add_up(pieces):
    total = pieces[0][...].astype(F32)
    for x in pieces[1:]:
        total = total + x[...].astype(F32)
    return total


def planes(ref):
    return [ref.at[n] for n in range(ref.shape[0])]


def features(ins, outs):
    dkv, weights = ins[:2]
    odq = ins[2:]
    attended, grads, feature = outs
    first = add_up(odq)
    second = add_up(planes(dkv)).astype(BF16)
    attended[...] = first[:DV].astype(BF16)
    all_grads = jnp.concatenate([first[DV:].astype(BF16), second], axis=0)
    grads[...] = all_grads
    feature[...] = dot(weights[...], all_grads, 1, 0).astype(BF16)


def outer(ins, outs):
    own, near, far, grads, far_grads, near_grads = ins
    pairs = [
        (own[...], grads[...]),
        (near[...], near_grads[0]),
        (far[0], far_grads[...]),
        (far[1], near_grads[1]),
    ]
    total = None
    for left, right in pairs:
        term = dot(left, right, 1, 1)
        total = term if total is None else total + term
    main = outs[0].shape[1]
    span = total.shape[1] - main
    block = 128
    row = lax.broadcasted_iota(jnp.int32, (block, block), 0)
    column = lax.broadcasted_iota(jnp.int32, (block, block), 1)
    spare = (row & (PAD - 1)) - SHARE
    source = row - (row & (PAD - 1)) + FOLD * spare
    picks = [
        jnp.where((spare >= 0) & (column == source + b), 1.0, 0.0).astype(BF16)
        for b in range(FOLD)
    ]
    tail = total[:, main:].astype(BF16)
    blank = jnp.zeros((block, span), F32)
    for n in range(total.shape[0] // block):
        rows = slice(n * block, (n + 1) * block)
        moved = [dot(e, tail[rows], 1, 0) for e in picks] + [blank]
        for c in range(2):
            lane = slice(c * DH, (c + 1) * DH)
            extra = jnp.concatenate(moved[2 * c : 2 * c + 2], axis=1)
            outs[0][rows, lane] = (total[rows, lane] + extra).astype(BF16)
        outs[0][rows, 2 * DH :] = total[rows, 2 * DH : main].astype(BF16)


def weight_sum(ins, outs, scale):
    total = add_up(planes(ins[0])) * scale
    span = 2 * DH + DV - total.shape[1]
    outs[0][...] = total[:SHARE, :DH]
    outs[1][...] = total[:SHARE, DH : 2 * DH]
    outs[2][:, : DV - span] = total[:SHARE, 2 * DH :]
    for r in range(SHARE):
        a, b = SHARE + r // FOLD, r % FOLD
        outs[2][r : r + 1, DV - span :] = total[a : a + 1, b * span : (b + 1) * span]


def feature_sum(ins, outs):
    outs[0][...] = add_up(planes(ins[0])).astype(BF16)


def spread(ins, outs):
    own, low, high, taps = ins
    width = own.shape[1]
    body = own[...].astype(F32)
    padded = jnp.concatenate([low[...].astype(F32), body, high[...].astype(F32)], axis=1)
    summed = body
    for t in range(5):
        start = width - (t - 2) * DILATION_STEP
        summed = summed + taps[:, t : t + 1] * padded[:, start : start + width]
    outs[0][...] = summed


def local(tokens, conv_taps, w_query, w_key, w_value, grad_out):
    x = tokens[0]
    rows, columns = x.shape
    k_count = lax.axis_size(KGROUP)
    bx, core, sx = (lax.axis_size(a) for a in ("bx", "core", "sx"))
    y = lax.axis_size(("yh", "yl"))
    rest = bx * y
    share = columns // (bx * core * sx * y)
    heads = lax.axis_size("heads")
    slice_width = columns // heads
    width = 2 * DH + DV
    packed = width - DV % DH

    low, high = shift_pair(x[rows - REACH :], x[:REACH], SEQ)
    weights = jnp.concatenate([w_query, w_key, w_value], axis=1)
    (inner,) = call(blend, [((rows, columns), F32)], x, conv_taps)
    blended, qdo, kv_all = call(
        project,
        [((rows, columns), BF16), ((DH + DV, rows), BF16), ((k_count, DH + DV, rows), BF16)],
        inner, low, high, conv_taps, weights, grad_out[0].T,
    )
    kv = exchange(kv_all, KGROUP)
    pair = swap(qdo, "sx")
    blended, pair = lax.optimization_barrier((blended, pair))
    quad = swap(jnp.stack([qdo, pair]), "yl")
    place = lax.axis_index(QGROUP).reshape(1).astype(jnp.int32)

    groups = blended.reshape(rows, bx, core, sx, y, share)
    groups = jnp.pad(groups, ((0, 0),) * 5 + ((0, PAD - share),))
    groups = groups.transpose(2, 3, 1, 4, 5, 0).reshape(core, sx, rest * PAD, rows)
    mine = lax.axis_index("core")
    side = lax.axis_index("sx")
    kept = lax.dynamic_index_in_dim(groups, mine, 0, False)
    count = lax.axis_size(QGROUP)
    (stats,) = call(
        statistics, [((count, count, 8, rows), F32)], place, kv, qdo, pair, quad,
        scalars=1,
    )
    given = lax.dynamic_index_in_dim(groups, 1 - mine, 0, False)
    stats, given = lax.optimization_barrier((stats, given))
    stats = exchange(stats, QGROUP)
    got = swap(given, "core")
    own = lax.dynamic_index_in_dim(kept, side, 0, False)
    near = lax.dynamic_index_in_dim(got, side, 0, False)
    crossing = jnp.stack(
        [
            lax.dynamic_index_in_dim(kept, 1 - side, 0, False),
            lax.dynamic_index_in_dim(got, 1 - side, 0, False),
        ]
    )

    stats, own, near, crossing = lax.optimization_barrier((stats, own, near, crossing))
    kept, nearby, sent, dkv = call(
        attend,
        [((DH + DV, rows), F32)] * 2
        + [((2, DH + DV, rows), BF16), ((k_count, DH + DV, rows), BF16)],
        place, kv, qdo, pair, quad, stats,
        scalars=1,
    )
    dkv = exchange(dkv, KGROUP)
    came = swap(sent, "yl")
    far = swap(crossing, "sx")
    kept, sent = call(
        fold,
        [((DH + DV, rows), F32), ((DH + DV, rows), BF16)],
        kept, nearby, came,
    )
    dkv, far = lax.optimization_barrier((dkv, far))
    attended, grads, feature = call(
        features,
        [((DV, rows), BF16), ((width, rows), BF16), ((columns, rows), BF16)],
        dkv, weights, kept, swap(sent, "sx"),
    )
    far_grads = swap(grads, "sx")
    near_grads = swap(jnp.stack([grads, far_grads]), "core")
    feature = exchange(feature.reshape(heads, slice_width, rows), "heads")
    (product,) = call(
        outer, [((rest * PAD, packed), BF16)],
        own, near, far, grads, far_grads, near_grads,
    )
    product = exchange(product.reshape(rest, PAD, packed), REST)

    (own,) = call(feature_sum, [((slice_width, rows), BF16)], feature)
    before, after = shift_pair(own, own, SEQ)
    taps = lax.dynamic_slice_in_dim(
        conv_taps, lax.axis_index("heads") * slice_width, slice_width, 1
    ).T
    (grad_tokens,) = call(spread, [((slice_width, rows), F32)], own, before, after, taps)
    scale = 1.0 / math.sqrt(bx * core * sx * y * rows)
    grad_query, grad_key, grad_value = call(
        lambda i, o: weight_sum(i, o, scale),
        [((share, DH), F32), ((share, DH), F32), ((share, DV), F32)],
        product,
    )
    return attended.T[None], grad_tokens.T[None], grad_query, grad_key, grad_value


def split(mesh):
    batch, heads, seq = mesh.devices.shape
    shape = (batch // 2, 2, heads, 2, seq // 4, 2)
    return Mesh(mesh.devices.reshape(shape), ("bx", "core", "heads", "sx", "yh", "yl"))


def solution(mesh):
    batch = ("bx", "core")
    whole = split(mesh)
    return jax.shard_map(
        local,
        mesh=whole,
        in_specs=(
            P(batch, SEQ, None),
            P(),
            P(None, "heads"),
            P(None, "heads"),
            P(None, "heads"),
            P(batch, SEQ, "heads"),
        ),
        out_specs=(
            P(batch, SEQ, "heads"),
            P(batch, SEQ, "heads"),
            P(batch + SEQ, "heads"),
            P(batch + SEQ, "heads"),
            P(batch + SEQ, "heads"),
        ),
        check_vma=False,
    )
```

```python
import math

import jax
import jax.numpy as jnp
from jax import lax
from jax.experimental import pallas as pl
from jax.experimental.pallas import tpu as pltpu
from jax.sharding import Mesh
from jax.sharding import PartitionSpec as P

DH = 128
DV = 192
DILATION_STEP = 4
REACH = 2 * DILATION_STEP
PAD = 16
SHARE = 12
FOLD = 3
VMEM = 16 << 20

F32 = jnp.float32
BF16 = jnp.bfloat16
SEQ = ("sx", "y")
QGROUP = "sx"
KGROUP = "y"
REST = ("bx", "y")


def dot(a, b, ca, cb):
    return lax.dot_general(a, b, (((ca,), (cb,)), ((), ())), preferred_element_type=F32)


def call(body, outs, *args, name, staged=None):
    count = len(args)

    def kernel(*refs):
        ins, results = refs[:count], refs[count : count + len(outs)]
        if staged is None:
            body(ins, results)
            return
        held, sems = refs[-2], refs[-1]
        target = results[-1]
        copies = []

        def ship(source, place):
            if copies:
                copies[-1].start()
            copies.append(
                pltpu.make_async_copy(source, target.at[place], sems.at[len(copies)])
            )

        body(ins, results[:-1], held, ship)
        copies[-1].start()
        for copy in copies:
            copy.wait()

    near = pl.BlockSpec(memory_space=pltpu.VMEM)
    specs = [near] * len(outs)
    scratch = []
    if staged is not None:
        shape, pieces = staged
        specs[-1] = pl.BlockSpec(memory_space=pl.ANY)
        scratch = [pltpu.VMEM(shape, outs[-1][1]), pltpu.SemaphoreType.DMA((pieces,))]
    return pl.pallas_call(
        kernel,
        out_shape=[jax.ShapeDtypeStruct(s, t) for s, t in outs],
        in_specs=[near] * count,
        out_specs=specs,
        scratch_shapes=scratch,
        name=name,
        compiler_params=pltpu.CompilerParams(vmem_limit_bytes=VMEM),
    )(*args)


def exchange(x, axis):
    return lax.all_to_all(x, axis, split_axis=0, concat_axis=0, tiled=True)


def swap(x, axis):
    return lax.ppermute(x, axis, [(0, 1), (1, 0)])


def shift_pair(low_source, high_source, axes):
    count = lax.axis_size(axes)
    forward = [(i, i + 1) for i in range(count - 1)]
    backward = [(j, i) for i, j in forward]
    return lax.ppermute(low_source, axes, forward), lax.ppermute(high_source, axes, backward)


def blend(ins, outs):
    tokens, taps = ins
    rows, columns = tokens.shape
    body = tokens[...].astype(F32)
    edge = jnp.zeros((REACH, columns), F32)
    padded = jnp.concatenate([edge, body, edge], axis=0)
    summed = body
    for t in range(5):
        summed = summed + taps[t : t + 1, :] * padded[t * DILATION_STEP : t * DILATION_STEP + rows]
    outs[0][...] = summed


def project(ins, outs):
    inner, low, high, taps, weights, do = ins
    blended_out, qdo, kv_out = outs
    rows, columns = inner.shape
    low = low[...].astype(F32)
    high = high[...].astype(F32)
    none = jnp.zeros((DILATION_STEP, columns), F32)
    first = taps[0:1] * low + jnp.concatenate([taps[1:2] * low[DILATION_STEP:], none], axis=0)
    last = taps[4:5] * high + jnp.concatenate([none, taps[3:4] * high[:DILATION_STEP]], axis=0)
    summed = jnp.concatenate(
        [inner[:REACH] + first, inner[REACH : rows - REACH], inner[rows - REACH :] + last], axis=0
    )
    blended = summed.astype(BF16)
    blended_out[...] = blended
    qkv = dot(blended, weights[...], 1, 0).T.astype(BF16)
    qdo[:DH] = qkv[:DH]
    qdo[DH:] = do[...]
    for n in range(kv_out.shape[0]):
        kv_out[n] = qkv[DH:]


def lanes(ref, first, last):
    return jnp.concatenate([ref[n, first:last] for n in range(ref.shape[0])], axis=1)


SCALE = 1.0 / math.sqrt(DH)


def statistics(ins, outs):
    kv, qdos = ins[0], ins[1:]
    stats, exponents, products = outs
    k_rows = lanes(kv, 0, DH).T
    v_rows = lanes(kv, DH, DH + DV).T
    width = qdos[0].shape[1]
    for m, qdo in enumerate(qdos):
        s = dot(k_rows, qdo[:DH], 1, 0) * SCALE
        top = jnp.max(s, axis=0, keepdims=True)
        e = jnp.exp(s - top)
        total = jnp.sum(e, axis=0, keepdims=True)
        dp = dot(v_rows, qdo[DH:], 1, 0)
        weighted = jnp.sum(e * dp, axis=0, keepdims=True)
        part = jnp.concatenate([top, total, weighted, jnp.zeros((5, width), F32)], axis=0)
        lane = slice(m * width, (m + 1) * width)
        stats[:, lane] = part
        exponents[:, lane] = e
        products[:, lane] = dp


def attend(ins, outs, dkv, ship):
    kv, exponents, products = ins[:3]
    blocks = len(outs)
    qdos, stats = ins[3 : 3 + blocks], ins[3 + blocks :]
    odq = outs
    kt = lanes(kv, 0, DH)
    vt = lanes(kv, DH, DH + DV)
    width = qdos[0].shape[1]
    dk = dv = None
    for m, qdo in enumerate(qdos):
        part = [stats[c][:, (m ^ c) * width : ((m ^ c) + 1) * width] for c in range(blocks)]
        top = part[0][0:1]
        for x in part[1:]:
            top = jnp.maximum(top, x[0:1])
        total = jnp.zeros_like(top)
        weighted = jnp.zeros_like(top)
        for x in part:
            factor = jnp.exp(x[0:1] - top)
            total = total + factor * x[1:2]
            weighted = weighted + factor * x[2:3]
        row_dots = weighted / total
        lane = slice(m * width, (m + 1) * width)
        a = exponents[:, lane] * (jnp.exp(part[0][0:1] - top) / total)
        ab = a.astype(BF16)
        ds = (a * (products[:, lane] - row_dots) * SCALE).astype(BF16)
        odq[m][:DV] = dot(vt, ab, 1, 0).astype(BF16)
        odq[m][DV:] = dot(kt, ds, 1, 0).astype(BF16)
        dk_m = dot(qdo[:DH], ds, 1, 1)
        dv_m = dot(qdo[DH:], ab, 1, 1)
        dk = dk_m if dk is None else dk + dk_m
        dv = dv_m if dv is None else dv + dv_m
    for n in range(dkv.shape[0]):
        dkv[n, :DH] = dk[:, n * width : (n + 1) * width].astype(BF16)
        dkv[n, DH:] = dv[:, n * width : (n + 1) * width].astype(BF16)
        ship(dkv.at[n], n)


def add_up(pieces):
    total = pieces[0][...].astype(F32)
    for x in pieces[1:]:
        total = total + x[...].astype(F32)
    return total


def planes(ref):
    return [ref.at[n] for n in range(ref.shape[0])]


def features(ins, outs):
    dkv, weights = ins[:2]
    odq = ins[2:]
    attended, grads, feature = outs
    first = add_up(odq)
    second = add_up(planes(dkv)).astype(BF16)
    attended[...] = first[:DV].astype(BF16)
    all_grads = jnp.concatenate([first[DV:].astype(BF16), second], axis=0)
    grads[...] = all_grads
    feature[...] = dot(weights[...], all_grads, 1, 0).astype(BF16)


def outer(ins, outs):
    own, near, far, grads, far_grads, near_grads = ins
    pairs = [
        (own[...], grads[...]),
        (near[...], near_grads[0]),
        (far[0], far_grads[...]),
        (far[1], near_grads[1]),
    ]
    total = None
    for left, right in pairs:
        term = dot(left, right, 1, 1)
        total = term if total is None else total + term
    main = outs[0].shape[1]
    span = total.shape[1] - main
    block = 128
    row = lax.broadcasted_iota(jnp.int32, (block, block), 0)
    column = lax.broadcasted_iota(jnp.int32, (block, block), 1)
    spare = (row & (PAD - 1)) - SHARE
    source = row - (row & (PAD - 1)) + FOLD * spare
    picks = [
        jnp.where((spare >= 0) & (column == source + b), 1.0, 0.0).astype(BF16)
        for b in range(FOLD)
    ]
    tail = total[:, main:].astype(BF16)
    blank = jnp.zeros((block, span), F32)
    for n in range(total.shape[0] // block):
        rows = slice(n * block, (n + 1) * block)
        moved = [dot(e, tail[rows], 1, 0) for e in picks] + [blank]
        for c in range(2):
            lane = slice(c * DH, (c + 1) * DH)
            extra = jnp.concatenate(moved[2 * c : 2 * c + 2], axis=1)
            outs[0][rows, lane] = (total[rows, lane] + extra).astype(BF16)
        outs[0][rows, 2 * DH :] = total[rows, 2 * DH : main].astype(BF16)


def weight_sum(ins, outs, scale):
    total = add_up(planes(ins[0])) * scale
    span = 2 * DH + DV - total.shape[1]
    outs[0][...] = total[:SHARE, :DH]
    outs[1][...] = total[:SHARE, DH : 2 * DH]
    outs[2][:, : DV - span] = total[:SHARE, 2 * DH :]
    for r in range(SHARE):
        a, b = SHARE + r // FOLD, r % FOLD
        outs[2][r : r + 1, DV - span :] = total[a : a + 1, b * span : (b + 1) * span]


def feature_sum(ins, outs):
    outs[0][...] = add_up(planes(ins[0])).astype(BF16)


def spread(ins, outs):
    own, low, high, taps = ins
    width = own.shape[1]
    body = own[...].astype(F32)
    padded = jnp.concatenate([low[...].astype(F32), body, high[...].astype(F32)], axis=1)
    summed = body
    for t in range(5):
        start = width - (t - 2) * DILATION_STEP
        summed = summed + taps[:, t : t + 1] * padded[:, start : start + width]
    outs[0][...] = summed


def local(tokens, conv_taps, w_query, w_key, w_value, grad_out):
    x = tokens[0]
    rows, columns = x.shape
    k_count = lax.axis_size(KGROUP)
    bx, core, sx, y = (lax.axis_size(a) for a in ("bx", "core", "sx", "y"))
    rest = bx * y
    share = columns // (bx * core * sx * y)
    heads = lax.axis_size("heads")
    slice_width = columns // heads
    width = 2 * DH + DV
    packed = width - DV % DH

    low, high = shift_pair(x[rows - REACH :], x[:REACH], SEQ)
    weights = jnp.concatenate([w_query, w_key, w_value], axis=1)
    (inner,) = call(blend, [((rows, columns), F32)], x, conv_taps, name="blend")
    blended, qdo, kv_all = call(
        project,
        [((rows, columns), BF16), ((DH + DV, rows), BF16), ((k_count, DH + DV, rows), BF16)],
        inner, low, high, conv_taps, weights, grad_out[0].T,
        name="project",
    )
    kv = exchange(kv_all, KGROUP)
    qdos = [qdo, swap(qdo, QGROUP)]

    groups = blended.reshape(rows, bx, core, sx, y, share)
    groups = jnp.pad(groups, ((0, 0),) * 5 + ((0, PAD - share),))
    groups = groups.transpose(2, 3, 1, 4, 5, 0).reshape(core, sx, rest * PAD, rows)
    mine = lax.axis_index("core")
    side = lax.axis_index("sx")
    kept = lax.dynamic_index_in_dim(groups, mine, 0, False)
    got = swap(lax.dynamic_index_in_dim(groups, 1 - mine, 0, False), "core")
    own = lax.dynamic_index_in_dim(kept, side, 0, False)
    near = lax.dynamic_index_in_dim(got, side, 0, False)
    crossing = jnp.stack(
        [
            lax.dynamic_index_in_dim(kept, 1 - side, 0, False),
            lax.dynamic_index_in_dim(got, 1 - side, 0, False),
        ]
    )
    kv, own, near, crossing = lax.optimization_barrier((kv, own, near, crossing))

    stats, exponents, products = call(
        statistics,
        [((8, sx * rows), F32)] + [((k_count * rows, sx * rows), F32)] * 2,
        kv, *qdos,
        name="statistics",
    )
    *odq, dkv = call(
        attend,
        [((DH + DV, rows), BF16)] * sx + [((k_count, DH + DV, rows), BF16)],
        kv, exponents, products, *qdos, stats, swap(stats, QGROUP),
        name="attend", staged=((k_count, DH + DV, rows), k_count),
    )
    dkv, far = lax.optimization_barrier((exchange(dkv, KGROUP), swap(crossing, "sx")))
    attended, grads, feature = call(
        features,
        [((DV, rows), BF16), ((width, rows), BF16), ((columns, rows), BF16)],
        dkv, weights, odq[0], swap(odq[1], QGROUP),
        name="features",
    )
    far_grads = swap(grads, "sx")
    near_grads = swap(jnp.stack([grads, far_grads]), "core")
    feature = exchange(feature.reshape(heads, slice_width, rows), "heads")
    (product,) = call(
        outer, [((rest * PAD, packed), BF16)],
        own, near, far, grads, far_grads, near_grads,
        name="outer",
    )
    product = exchange(product.reshape(rest, PAD, packed), REST)

    (own,) = call(feature_sum, [((slice_width, rows), BF16)], feature, name="feature_sum")
    before, after = shift_pair(own, own, SEQ)
    taps = lax.dynamic_slice_in_dim(
        conv_taps, lax.axis_index("heads") * slice_width, slice_width, 1
    ).T
    (grad_tokens,) = call(
        spread, [((slice_width, rows), F32)], own, before, after, taps, name="spread"
    )
    scale = 1.0 / math.sqrt(bx * core * sx * y * rows)
    grad_query, grad_key, grad_value = call(
        lambda i, o: weight_sum(i, o, scale),
        [((share, DH), F32), ((share, DH), F32), ((share, DV), F32)],
        product,
        name="weight_sum",
    )
    return attended.T[None], grad_tokens.T[None], grad_query, grad_key, grad_value


def split(mesh):
    batch, heads, seq = mesh.devices.shape
    shape = (batch // 2, 2, heads, 2, seq // 2)
    return Mesh(mesh.devices.reshape(shape), ("bx", "core", "heads", "sx", "y"))


def solution(mesh):
    batch = ("bx", "core")
    whole = split(mesh)
    return jax.shard_map(
        local,
        mesh=whole,
        in_specs=(
            P(batch, SEQ, None),
            P(),
            P(None, "heads"),
            P(None, "heads"),
            P(None, "heads"),
            P(batch, SEQ, "heads"),
        ),
        out_specs=(
            P(batch, SEQ, "heads"),
            P(batch, SEQ, "heads"),
            P(batch + SEQ, "heads"),
            P(batch + SEQ, "heads"),
            P(batch + SEQ, "heads"),
        ),
        check_vma=False,
    )
```

```python
import math

import jax
import jax.numpy as jnp
from jax import lax
from jax.experimental import pallas as pl
from jax.experimental.pallas import tpu as pltpu
from jax.sharding import Mesh
from jax.sharding import PartitionSpec as P

DH = 128
DV = 192
DILATION_STEP = 4
REACH = 2 * DILATION_STEP
PAD = 16
SHARE = 12
FOLD = 3
VMEM = 16 << 20

F32 = jnp.float32
BF16 = jnp.bfloat16
SEQ = ("sx", "y")
QGROUP = "sx"
KGROUP = "y"
REST = ("bx", "y")


def dot(a, b, ca, cb):
    return lax.dot_general(a, b, (((ca,), (cb,)), ((), ())), preferred_element_type=F32)


def call(body, outs, *args, name, staged=None):
    count = len(args)

    def kernel(*refs):
        ins, results = refs[:count], refs[count : count + len(outs)]
        if staged is None:
            body(ins, results)
            return
        held, sems = refs[-2], refs[-1]
        target = results[-1]
        copies = []

        def ship(source, place):
            if copies:
                copies[-1].start()
            copies.append(
                pltpu.make_async_copy(source, target.at[place], sems.at[len(copies)])
            )

        body(ins, results[:-1], held, ship)
        copies[-1].start()
        for copy in copies:
            copy.wait()

    near = pl.BlockSpec(memory_space=pltpu.VMEM)
    specs = [near] * len(outs)
    scratch = []
    if staged is not None:
        shape, pieces = staged
        specs[-1] = pl.BlockSpec(memory_space=pl.ANY)
        scratch = [pltpu.VMEM(shape, outs[-1][1]), pltpu.SemaphoreType.DMA((pieces,))]
    return pl.pallas_call(
        kernel,
        out_shape=[jax.ShapeDtypeStruct(s, t) for s, t in outs],
        in_specs=[near] * count,
        out_specs=specs,
        scratch_shapes=scratch,
        name=name,
        compiler_params=pltpu.CompilerParams(vmem_limit_bytes=VMEM),
    )(*args)


def exchange(x, axis):
    return lax.all_to_all(x, axis, split_axis=0, concat_axis=0, tiled=True)


def swap(x, axis):
    return lax.ppermute(x, axis, [(0, 1), (1, 0)])


def shift_pair(low_source, high_source, axes):
    count = lax.axis_size(axes)
    forward = [(i, i + 1) for i in range(count - 1)]
    backward = [(j, i) for i, j in forward]
    return lax.ppermute(low_source, axes, forward), lax.ppermute(high_source, axes, backward)


def blend(ins, outs):
    tokens, taps = ins
    rows, columns = tokens.shape
    body = tokens[...].astype(F32)
    edge = jnp.zeros((REACH, columns), F32)
    padded = jnp.concatenate([edge, body, edge], axis=0)
    summed = body
    for t in range(5):
        summed = summed + taps[t : t + 1, :] * padded[t * DILATION_STEP : t * DILATION_STEP + rows]
    outs[0][...] = summed


def project(ins, outs):
    inner, low, high, taps, weights, do = ins
    blended_out, qdo, kv_out = outs
    rows, columns = inner.shape
    low = low[...].astype(F32)
    high = high[...].astype(F32)
    none = jnp.zeros((DILATION_STEP, columns), F32)
    first = taps[0:1] * low + jnp.concatenate([taps[1:2] * low[DILATION_STEP:], none], axis=0)
    last = taps[4:5] * high + jnp.concatenate([none, taps[3:4] * high[:DILATION_STEP]], axis=0)
    summed = jnp.concatenate(
        [inner[:REACH] + first, inner[REACH : rows - REACH], inner[rows - REACH :] + last], axis=0
    )
    blended = summed.astype(BF16)
    blended_out[...] = blended
    qkv = dot(blended, weights[...], 1, 0).T.astype(BF16)
    qdo[:DH] = qkv[:DH]
    qdo[DH:] = do[...]
    for n in range(kv_out.shape[0]):
        kv_out[n] = qkv[DH:]


def lanes(ref, first, last):
    return jnp.concatenate([ref[n, first:last] for n in range(ref.shape[0])], axis=1)


SCALE = 1.0 / math.sqrt(DH)


def statistics(ins, outs):
    kv, qdos = ins[0], ins[1:]
    stats, exponents, products = outs
    k_rows = lanes(kv, 0, DH).T
    v_rows = lanes(kv, DH, DH + DV).T
    width = qdos[0].shape[1]
    for m, qdo in enumerate(qdos):
        s = dot(k_rows, qdo[:DH], 1, 0) * SCALE
        top = jnp.max(s, axis=0, keepdims=True)
        e = jnp.exp(s - top)
        total = jnp.sum(e, axis=0, keepdims=True)
        dp = dot(v_rows, qdo[DH:], 1, 0)
        weighted = jnp.sum(e * dp, axis=0, keepdims=True)
        part = jnp.concatenate([top, total, weighted, jnp.zeros((5, width), F32)], axis=0)
        lane = slice(m * width, (m + 1) * width)
        stats[:, lane] = part
        exponents[:, lane] = e
        products[:, lane] = dp


def attend(ins, outs, dkv, ship):
    kv, exponents, products = ins[:3]
    blocks = len(outs)
    qdos, stats = ins[3 : 3 + blocks], ins[3 + blocks :]
    odq = outs
    kt = lanes(kv, 0, DH)
    vt = lanes(kv, DH, DH + DV)
    width = qdos[0].shape[1]
    dk = dv = None
    for m, qdo in enumerate(qdos):
        part = [stats[c][:, (m ^ c) * width : ((m ^ c) + 1) * width] for c in range(blocks)]
        top = part[0][0:1]
        for x in part[1:]:
            top = jnp.maximum(top, x[0:1])
        total = jnp.zeros_like(top)
        weighted = jnp.zeros_like(top)
        for x in part:
            factor = jnp.exp(x[0:1] - top)
            total = total + factor * x[1:2]
            weighted = weighted + factor * x[2:3]
        row_dots = weighted / total
        lane = slice(m * width, (m + 1) * width)
        a = exponents[:, lane] * (jnp.exp(part[0][0:1] - top) / total)
        ab = a.astype(BF16)
        ds = (a * (products[:, lane] - row_dots) * SCALE).astype(BF16)
        odq[m][:DV] = dot(vt, ab, 1, 0).astype(BF16)
        odq[m][DV:] = dot(kt, ds, 1, 0).astype(BF16)
        dk_m = dot(qdo[:DH], ds, 1, 1)
        dv_m = dot(qdo[DH:], ab, 1, 1)
        dk = dk_m if dk is None else dk + dk_m
        dv = dv_m if dv is None else dv + dv_m
    for n in range(dkv.shape[0]):
        dkv[n, :DH] = dk[:, n * width : (n + 1) * width].astype(BF16)
        dkv[n, DH:] = dv[:, n * width : (n + 1) * width].astype(BF16)
        ship(dkv.at[n], n)


def add_up(pieces):
    total = pieces[0][...].astype(F32)
    for x in pieces[1:]:
        total = total + x[...].astype(F32)
    return total


def planes(ref):
    return [ref.at[n] for n in range(ref.shape[0])]


def features(ins, outs):
    dkv, weights = ins[:2]
    odq = ins[2:]
    attended, grads, feature = outs
    first = add_up(odq)
    second = add_up(planes(dkv)).astype(BF16)
    attended[...] = first[:DV].astype(BF16)
    all_grads = jnp.concatenate([first[DV:].astype(BF16), second], axis=0)
    grads[...] = all_grads
    feature[...] = dot(weights[...], all_grads, 1, 0).astype(BF16)


def outer_here(ins, outs):
    own, far, grads, far_grads = ins
    outs[0][...] = dot(own[...], grads[...], 1, 1) + dot(far[0], far_grads[...], 1, 1)


def outer(ins, outs):
    near, far, near_grads, here = ins
    total = here[...] + dot(near[...], near_grads[0], 1, 1)
    total = total + dot(far[1], near_grads[1], 1, 1)
    main = outs[0].shape[1]
    span = total.shape[1] - main
    block = 128
    row = lax.broadcasted_iota(jnp.int32, (block, block), 0)
    column = lax.broadcasted_iota(jnp.int32, (block, block), 1)
    spare = (row & (PAD - 1)) - SHARE
    source = row - (row & (PAD - 1)) + FOLD * spare
    picks = [
        jnp.where((spare >= 0) & (column == source + b), 1.0, 0.0).astype(BF16)
        for b in range(FOLD)
    ]
    tail = total[:, main:].astype(BF16)
    blank = jnp.zeros((block, span), F32)
    for n in range(total.shape[0] // block):
        rows = slice(n * block, (n + 1) * block)
        moved = [dot(e, tail[rows], 1, 0) for e in picks] + [blank]
        for c in range(2):
            lane = slice(c * DH, (c + 1) * DH)
            extra = jnp.concatenate(moved[2 * c : 2 * c + 2], axis=1)
            outs[0][rows, lane] = (total[rows, lane] + extra).astype(BF16)
        outs[0][rows, 2 * DH :] = total[rows, 2 * DH : main].astype(BF16)


def weight_sum(ins, outs, scale):
    total = add_up(planes(ins[0])) * scale
    span = 2 * DH + DV - total.shape[1]
    outs[0][...] = total[:SHARE, :DH]
    outs[1][...] = total[:SHARE, DH : 2 * DH]
    outs[2][:, : DV - span] = total[:SHARE, 2 * DH :]
    for r in range(SHARE):
        a, b = SHARE + r // FOLD, r % FOLD
        outs[2][r : r + 1, DV - span :] = total[a : a + 1, b * span : (b + 1) * span]


def feature_sum(ins, outs):
    outs[0][...] = add_up(planes(ins[0])).astype(BF16)


def spread(ins, outs):
    own, low, high, taps = ins
    width = own.shape[1]
    body = own[...].astype(F32)
    padded = jnp.concatenate([low[...].astype(F32), body, high[...].astype(F32)], axis=1)
    summed = body
    for t in range(5):
        start = width - (t - 2) * DILATION_STEP
        summed = summed + taps[:, t : t + 1] * padded[:, start : start + width]
    outs[0][...] = summed


def local(tokens, conv_taps, w_query, w_key, w_value, grad_out):
    x = tokens[0]
    rows, columns = x.shape
    k_count = lax.axis_size(KGROUP)
    bx, core, sx, y = (lax.axis_size(a) for a in ("bx", "core", "sx", "y"))
    rest = bx * y
    share = columns // (bx * core * sx * y)
    heads = lax.axis_size("heads")
    slice_width = columns // heads
    width = 2 * DH + DV
    packed = width - DV % DH

    low, high = shift_pair(x[rows - REACH :], x[:REACH], SEQ)
    weights = jnp.concatenate([w_query, w_key, w_value], axis=1)
    (inner,) = call(blend, [((rows, columns), F32)], x, conv_taps, name="blend")
    blended, qdo, kv_all = call(
        project,
        [((rows, columns), BF16), ((DH + DV, rows), BF16), ((k_count, DH + DV, rows), BF16)],
        inner, low, high, conv_taps, weights, grad_out[0].T,
        name="project",
    )
    kv = exchange(kv_all, KGROUP)
    qdos = [qdo, swap(qdo, QGROUP)]

    groups = blended.reshape(rows, bx, core, sx, y, share)
    groups = jnp.pad(groups, ((0, 0),) * 5 + ((0, PAD - share),))
    groups = groups.transpose(2, 3, 1, 4, 5, 0).reshape(core, sx, rest * PAD, rows)
    mine = lax.axis_index("core")
    side = lax.axis_index("sx")
    kept = lax.dynamic_index_in_dim(groups, mine, 0, False)
    got = swap(lax.dynamic_index_in_dim(groups, 1 - mine, 0, False), "core")
    own = lax.dynamic_index_in_dim(kept, side, 0, False)
    near = lax.dynamic_index_in_dim(got, side, 0, False)
    crossing = jnp.stack(
        [
            lax.dynamic_index_in_dim(kept, 1 - side, 0, False),
            lax.dynamic_index_in_dim(got, 1 - side, 0, False),
        ]
    )
    kv, own, near, crossing = lax.optimization_barrier((kv, own, near, crossing))

    stats, exponents, products = call(
        statistics,
        [((8, sx * rows), F32)] + [((k_count * rows, sx * rows), F32)] * 2,
        kv, *qdos,
        name="statistics",
    )
    *odq, dkv = call(
        attend,
        [((DH + DV, rows), BF16)] * sx + [((k_count, DH + DV, rows), BF16)],
        kv, exponents, products, *qdos, stats, swap(stats, QGROUP),
        name="attend", staged=((k_count, DH + DV, rows), k_count),
    )
    dkv, far = lax.optimization_barrier((exchange(dkv, KGROUP), swap(crossing, "sx")))
    attended, grads, feature = call(
        features,
        [((DV, rows), BF16), ((width, rows), BF16), ((columns, rows), BF16)],
        dkv, weights, odq[0], swap(odq[1], QGROUP),
        name="features",
    )
    far_grads = swap(grads, "sx")
    near_grads = swap(jnp.stack([grads, far_grads]), "core")
    feature = exchange(feature.reshape(heads, slice_width, rows), "heads")
    (here,) = call(
        outer_here, [((rest * PAD, width), F32)],
        own, far, grads, far_grads,
        name="outer_here",
    )
    (product,) = call(
        outer, [((rest * PAD, packed), BF16)],
        near, far, near_grads, here,
        name="outer",
    )
    product = exchange(product.reshape(rest, PAD, packed), REST)

    (own,) = call(feature_sum, [((slice_width, rows), BF16)], feature, name="feature_sum")
    before, after = shift_pair(own, own, SEQ)
    taps = lax.dynamic_slice_in_dim(
        conv_taps, lax.axis_index("heads") * slice_width, slice_width, 1
    ).T
    (grad_tokens,) = call(
        spread, [((slice_width, rows), F32)], own, before, after, taps, name="spread"
    )
    scale = 1.0 / math.sqrt(bx * core * sx * y * rows)
    grad_query, grad_key, grad_value = call(
        lambda i, o: weight_sum(i, o, scale),
        [((share, DH), F32), ((share, DH), F32), ((share, DV), F32)],
        product,
        name="weight_sum",
    )
    return attended.T[None], grad_tokens.T[None], grad_query, grad_key, grad_value


def split(mesh):
    batch, heads, seq = mesh.devices.shape
    shape = (batch // 2, 2, heads, 2, seq // 2)
    return Mesh(mesh.devices.reshape(shape), ("bx", "core", "heads", "sx", "y"))


def solution(mesh):
    batch = ("bx", "core")
    whole = split(mesh)
    return jax.shard_map(
        local,
        mesh=whole,
        in_specs=(
            P(batch, SEQ, None),
            P(),
            P(None, "heads"),
            P(None, "heads"),
            P(None, "heads"),
            P(batch, SEQ, "heads"),
        ),
        out_specs=(
            P(batch, SEQ, "heads"),
            P(batch, SEQ, "heads"),
            P(batch + SEQ, "heads"),
            P(batch + SEQ, "heads"),
            P(batch + SEQ, "heads"),
        ),
        check_vma=False,
    )
```
